32 devices in a mesh: dp: 4 (over y, x), space: 8 (over z, core).
Axes of the slice: x: 2, y: 2, z: 4, core: 2. Of those that a mesh axis runs over, the one named last changes fastest.
Arguments:
- voxel_feats: bfloat16 [4, 1024, 256], P('dp', 'space'), may hold values from -6 to 6
- neighbours: int32 [4, 1024, 6], P('dp', 'space'), may hold values from 0 to 192
- wanted_rows: int32 [4, 8, 8, 8], P('dp', 'space'), may hold values from 0 to 127
- live_counts: int32 [4, 8], P('dp'), may hold values from 1 to 128, 768 in all within a row
- block_choice: int32 [4, 16, 4], P('dp', 'space'), may hold values from 0 to 15, all different within a row
- conv_weight: bfloat16 [7, 256, 512], P(None, 'space'), may hold values from -0.125 to 0.125
- norm_gain: float32 [512], replicated, may hold values from 0.1 to 1.9
- input_weight: bfloat16 [512, 2304], P('space'), may hold values from -5 to 5
- output_weight: bfloat16 [768, 512], P('space'), may hold values from -0.21875 to 0.21875
- cotangent: bfloat16 [4, 1024, 512], P('dp', 'space'), may hold values from -6 to 6
Outputs:
- layer_output: bfloat16 [4, 1024, 512], P('dp', 'space')
- output_grad: float32 [768, 512], P('space')
The draws below stay inside these ranges and needn't reach their ends.
Inputs may be any that keep to these rules, and one draw needn't show every extreme that they name: `neighbours`: an entry below 128 names a row of the device's own shard, entry 128 + p * 8 + c names the row taken from peer p in slot c, and the largest value names an absent neighbour. `wanted_rows`: places within the peer's shard. `block_choice`: each row names distinct blocks.
All inputs are finite; a program needn't handle non-finite values.
Results may differ from the reference program's by a relative error of at most 0.025.
Values may be sent and summed in bfloat16 or wider, within the bound.
No kernel may reach another device: no remote copies, remote signals or barrier semaphores. Data moves between devices by JAX's collectives and lax.ppermute only.
A program may use at most 64 MiB of HBM per device.

```python
import math
import jax
import jax.numpy as jnp
import numpy as np
from jax import lax

CIN = 256
WIDTH = 512
ATT = 768
HEADS = 12
HEAD_DIM = 64
TAPS = 7
TOK_DEV = 128
BLK = 64
CAP = 8
SEL = 4
SHAPES = 4
TOKENS = 1024
BLOCKS = 16
N_SPACE = 8


def draw_input_weight(key, part):
    initial = jnp.clip(jax.random.normal(key, (WIDTH, 3 * ATT), jnp.float32), -4.0, 4.0) * WIDTH ** (-0.5)
    aligned = -4.0 * initial[:, :ATT] + initial[:, ATT:2 * ATT]
    combined = jnp.concatenate([initial[:, :ATT], aligned, initial[:, 2 * ATT:]], axis=1)
    return combined.astype(jnp.bfloat16)


def draw_voxel_feats(key, part):
    shard_count = TOKENS // TOK_DEV
    shape_key = jax.random.fold_in(key, 17)
    region_key = jax.random.fold_in(key, 29)
    jitter_key = jax.random.fold_in(key, 41)
    shape_common = 0.65 * jax.random.normal(shape_key, (SHAPES, 1, 1, CIN), jnp.float32)
    region_part = 0.65 * jax.random.normal(region_key, (SHAPES, shard_count, 1, CIN), jnp.float32)
    jitter = 0.35 * jax.random.normal(jitter_key, (SHAPES, shard_count, TOK_DEV, CIN), jnp.float32)
    combined = (shape_common + region_part + jitter).reshape(SHAPES, TOKENS, CIN)
    return jnp.clip(combined, -6.0, 6.0).astype(jnp.bfloat16)


def place_ends(array, rng, least, high):
    shape = array.shape
    spot = [jax.random.randint(jax.random.fold_in(rng, axis), (), 0, shape[axis]) for axis in range(len(shape))]
    array = array.at[tuple(spot)].set(least)
    longest = shape.index(max(shape))
    spot[longest] = (spot[longest] + 1) % shape[longest]
    return array.at[tuple(spot)].set(high)


def level_of(key, shape, shards, smallest, largest):
    def one(position, parts):
        heights = jax.random.uniform(jax.random.fold_in(jax.random.fold_in(key, 6), position), (parts,), jnp.float32, smallest / len(shards), largest / len(shards))
        return jnp.repeat(jnp.exp(heights), shape[position] // parts).reshape((-1,) + (1,) * (len(shape) - position - 1))

    gain = one(*shards[0])
    for cut in shards[1:]:
        gain = gain * one(*cut)
    return gain


def distinct(rng, rows, number_of, top, lift):
    ranking = jax.random.permutation(jax.random.fold_in(rng, 1), number_of)
    pull = ranking
    for power in range(3):
        pull = pull * pull // number_of
    pull = pull * lift // number_of
    tickets = jax.random.randint(jax.random.fold_in(rng, 2), (rows, number_of), 0, 4096) + pull
    holders = jax.random.permutation(jax.random.fold_in(rng, 3), rows)[jnp.arange(number_of) % rows]
    tickets = jnp.where(jnp.arange(rows)[:, None] == holders[None, :], 1 << 14, tickets)
    priority = tickets * number_of + jnp.arange(number_of)
    return lax.top_k(priority.astype(jnp.int32), top)[1].astype(jnp.int32)


def profile(amount, total, bound, lean):
    loads = [(1 << 20) // math.isqrt(rank ** lean) + 1 for rank in range(2, amount + 1)]
    rest, given = total - bound - (amount - 1), [1] * (amount - 1)
    while rest > 0:
        free = [i for i in range(amount - 1) if given[i] < bound]
        whole, remaining = sum([loads[i] for i in free]), rest
        for i in free:
            addition = min(bound - given[i], max(1, remaining * loads[i] // whole), rest)
            given[i] = given[i] + addition
            rest = rest - addition
    return np.array([bound] + given)


def ragged_sizes(rng, count, total, reach, skew):
    if count == 2:
        one = jax.random.randint(rng, (), max(1, total - reach), min(reach, total - 1) + 1)
        return jnp.stack([one, total - one])
    sizes = jnp.asarray(profile(count, total, reach, skew), jnp.int32)
    pairs = (count - 1) // 2
    source_of, sink = sizes[1:1 + 2 * pairs:2], sizes[2:2 + 2 * pairs:2]
    slack = jnp.minimum(source_of - 1, reach - sink)
    passed = jax.random.randint(jax.random.fold_in(rng, 1), (pairs,), 0, 1 << 20) % (slack + 1)
    sizes = sizes.at[1:1 + 2 * pairs:2].set(source_of - passed).at[2:2 + 2 * pairs:2].set(sink + passed)
    return sizes[jax.random.permutation(jax.random.fold_in(rng, 2), count)]


def scatter_about(rng, extent, width, bound, split=(), held_as=jnp.bfloat16):
    loudness = level_of(rng, extent, split, -0.22, 0.18) if split else 1.0
    values = jax.random.normal(rng, extent, jnp.float32) * width * loudness
    return jnp.minimum(jnp.maximum(values, -bound), bound).astype(held_as)


def setup_inputs(seed: int = 0) -> dict:
    key_list = jax.random.split(jax.random.key(seed), 11)
    voxel_feats = draw_voxel_feats(jax.random.fold_in(key_list[10], 71), 0)
    neighbours = place_ends(jax.random.randint(key_list[1], (SHAPES, TOKENS, TAPS - 1), 0, TOK_DEV + N_SPACE * CAP + 1), jax.random.fold_in(key_list[1], 1), 0, TOK_DEV + N_SPACE * CAP).astype(jnp.int32)
    wanted_rows = place_ends(jax.random.randint(key_list[2], (SHAPES, N_SPACE, N_SPACE, CAP), 0, TOK_DEV), jax.random.fold_in(key_list[2], 1), 0, TOK_DEV - 1).astype(jnp.int32)
    live_counts = jax.vmap(lambda own: ragged_sizes(own, N_SPACE, TOKENS * 3 // 4, TOK_DEV, 2))(jax.random.split(key_list[3], SHAPES)).reshape((SHAPES, N_SPACE)).astype(jnp.int32)
    block_choice = distinct(key_list[4], SHAPES * BLOCKS, BLOCKS, SEL, 0).reshape((SHAPES, BLOCKS, SEL))
    conv_weight = scatter_about(key_list[5], (TAPS, CIN, WIDTH), (TAPS * CIN) ** -0.5, 0.125, ((1, 8),))
    norm_gain = jnp.clip(1.0 + 0.18 * jax.random.normal(key_list[6], (WIDTH,), jnp.float32), 0.1, 1.9)
    input_weight = draw_input_weight(jax.random.fold_in(key_list[10], 71), 0)
    output_weight = scatter_about(key_list[8], (ATT, WIDTH), ATT ** -0.5, 0.21875, ((0, 8),))
    cotangent = scatter_about(key_list[9], (SHAPES, TOKENS, WIDTH), 1.0, 6.0, ((0, 4), (1, 8)))
    return {"voxel_feats": voxel_feats, "neighbours": neighbours, "wanted_rows": wanted_rows, "live_counts": live_counts, "block_choice": block_choice, "conv_weight": conv_weight, "norm_gain": norm_gain, "input_weight": input_weight, "output_weight": output_weight, "cotangent": cotangent}


def attend(query, keys, values, key_live, short_keys, short_values):
    scale = HEAD_DIM ** (-0.5)
    query = query.astype(jnp.float32)
    near = jnp.einsum('bqhd,bkhd->bhqk', query, keys.astype(jnp.float32)) * scale
    near = jnp.where(key_live[:, None, None, :], near, -1e+30)
    far = jnp.einsum('bqhd,bshd->bhqs', query, short_keys.astype(jnp.float32)) * scale
    scores = jnp.concatenate([near, far], axis=-1)
    highest = lax.optimization_barrier(jnp.max(scores, axis=-1, keepdims=True))
    weights = jnp.exp(scores - highest)
    weights = (weights / lax.optimization_barrier(jnp.sum(weights, axis=-1, keepdims=True))).astype(jnp.bfloat16).astype(jnp.float32)
    mixed = jnp.einsum('bhqk,bkhd->bqhd', weights[..., :BLK], values.astype(jnp.float32))
    return mixed + jnp.einsum('bhqs,bshd->bqhd', weights[..., BLK:], short_values.astype(jnp.float32))

def one_shape(items, conv_weight, norm_gain, input_weight, output_weight):
    rows, index_map, lists, counts, chosen, upstream = items
    flat_weight = conv_weight.reshape(TAPS * CIN, WIDTH)
    positions = jnp.arange(TOKENS, dtype=jnp.int32)
    shard_of = positions // TOK_DEV
    place = positions % TOK_DEV
    owners = jnp.arange(N_SPACE, dtype=jnp.int32)[None, :, None] * TOK_DEV
    fetched = (owners + lists).reshape(N_SPACE, N_SPACE * CAP).astype(jnp.int32)
    absent = jnp.full((N_SPACE, 1), TOKENS, jnp.int32)
    lookup = jnp.concatenate([positions.reshape(N_SPACE, TOK_DEV), fetched, absent], axis=1)
    global_ids = jnp.take_along_axis(lookup, index_map.reshape(N_SPACE, TOK_DEV * (TAPS - 1)), axis=1)
    global_ids = global_ids.reshape(TOKENS, TAPS - 1)
    padded = jnp.concatenate([rows, jnp.zeros((1, CIN), jnp.bfloat16)], axis=0)
    taps = jnp.concatenate([rows[:, None, :], padded[global_ids]], axis=1).reshape(TOKENS, TAPS * CIN)
    live = place < counts[shard_of]
    live_f = live.astype(jnp.float32)
    hidden = jnp.dot(taps, flat_weight, preferred_element_type=jnp.float32) * live_f[:, None]
    power = lax.optimization_barrier(jnp.mean(hidden * hidden, axis=-1, keepdims=True))
    normed = (hidden * lax.rsqrt(power + 1e-06) * norm_gain).astype(jnp.bfloat16)
    projected = jnp.dot(normed, input_weight, preferred_element_type=jnp.float32).astype(jnp.bfloat16)
    query = projected[:, :ATT].reshape(BLOCKS, BLK, HEADS, HEAD_DIM)
    keys = projected[:, ATT:2 * ATT]
    values = projected[:, 2 * ATT:]
    block_live = live_f.reshape(BLOCKS, BLK)
    divisor = jnp.maximum(lax.optimization_barrier(jnp.sum(block_live, axis=1)), 1.0)[:, None]
    short_keys = (lax.optimization_barrier(jnp.sum(keys.astype(jnp.float32).reshape(BLOCKS, BLK, ATT) * block_live[:, :, None], axis=1)) / divisor).astype(jnp.bfloat16)
    short_values = (lax.optimization_barrier(jnp.sum(values.astype(jnp.float32).reshape(BLOCKS, BLK, ATT) * block_live[:, :, None], axis=1)) / divisor).astype(jnp.bfloat16)
    picked_keys = short_keys[chosen].reshape(BLOCKS, SEL, HEADS, HEAD_DIM)
    picked_values = short_values[chosen].reshape(BLOCKS, SEL, HEADS, HEAD_DIM)
    mixed = attend(query, keys.reshape(BLOCKS, BLK, HEADS, HEAD_DIM), values.reshape(BLOCKS, BLK, HEADS, HEAD_DIM), live.reshape(BLOCKS, BLK), picked_keys, picked_values)
    attended = (mixed.reshape(TOKENS, ATT) * live_f[:, None]).astype(jnp.bfloat16)
    layer = (hidden + jnp.dot(attended, output_weight, preferred_element_type=jnp.float32)).astype(jnp.bfloat16)
    grad_term = jnp.dot(attended.T, upstream, preferred_element_type=jnp.float32)
    return (layer, grad_term)

def reference(voxel_feats, neighbours, wanted_rows, live_counts, block_choice, conv_weight, norm_gain, input_weight, output_weight, cotangent):

    def runner(items):
        return one_shape(items, conv_weight, norm_gain, input_weight, output_weight)
    layers, terms = lax.map(runner, (voxel_feats, neighbours, wanted_rows, live_counts, block_choice, cotangent))
    factor = (SHAPES * TOKENS) ** (-0.5)
    return (layers, lax.optimization_barrier(jnp.sum(terms, axis=0)) * factor)
```

```python
import functools

import jax
import jax.numpy as jnp
from jax import lax
from jax.experimental import pallas as pl
from jax.experimental.pallas import tpu as pltpu
from jax.sharding import PartitionSpec as P

HEADS = 12
HEAD_DIM = 64
BLK = 64
SEL = 4


def attend(query, keys, values, key_live, short_keys, short_values):
    scale = HEAD_DIM ** (-0.5)
    near = jnp.einsum("bqhd,bkhd->bhqk", query, keys, preferred_element_type=jnp.float32) * scale
    near = jnp.where(key_live[:, None, None, :], near, -1e30)
    far = (
        jnp.einsum("bqhd,bshd->bhqs", query, short_keys, preferred_element_type=jnp.float32) * scale
    )
    scores = jnp.concatenate([near, far], axis=-1)
    highest = jnp.max(scores, axis=-1, keepdims=True)
    weights = jnp.exp(scores - highest)
    weights = (weights / jnp.sum(weights, axis=-1, keepdims=True)).astype(jnp.bfloat16)
    mixed = jnp.einsum(
        "bhqk,bkhd->bqhd", weights[..., :BLK], values, preferred_element_type=jnp.float32
    )
    return mixed + jnp.einsum(
        "bhqs,bshd->bqhd", weights[..., BLK:], short_values, preferred_element_type=jnp.float32
    )


def general_shards(
    voxel_feats,
    neighbours,
    wanted_rows,
    live_counts,
    block_choice,
    conv_weight,
    norm_gain,
    input_weight,
    output_weight,
    cotangent,
):
    space_count = lax.axis_size("space")
    position = lax.axis_index("space")
    own_rows = voxel_feats[0]
    shard_rows = own_rows.shape[0]
    index_map = neighbours[0]
    zero_row = jnp.zeros((1, own_rows.shape[1]), jnp.bfloat16)
    requested = lax.all_to_all(wanted_rows[0, 0], "space", split_axis=0, concat_axis=0, tiled=True)
    answers = own_rows[requested]
    arrived = lax.all_to_all(answers, "space", split_axis=0, concat_axis=0, tiled=True)
    padded = jnp.concatenate([own_rows, arrived.reshape(-1, own_rows.shape[1]), zero_row], axis=0)
    gathered_taps = padded[index_map]
    table = jnp.concatenate([own_rows[:, None, :], gathered_taps], axis=1)
    columns = table
    hidden = jnp.einsum(
        "tkr,kro->to",
        columns,
        lax.all_gather(conv_weight, "space", axis=1, tiled=True),
        preferred_element_type=jnp.float32,
    )
    live_count = lax.dynamic_index_in_dim(live_counts[0], position, keepdims=False)
    live = jnp.arange(shard_rows, dtype=jnp.int32) < live_count
    live_f = live.astype(jnp.float32)
    hidden = hidden * live_f[:, None]
    power = jnp.mean(hidden * hidden, axis=-1, keepdims=True)
    normed = (hidden * lax.rsqrt(power + 1e-06) * norm_gain).astype(jnp.bfloat16)
    columns = normed
    projected = jnp.dot(
        columns,
        lax.all_gather(input_weight, "space", axis=0, tiled=True),
        preferred_element_type=jnp.float32,
    ).astype(jnp.bfloat16)
    att_width = input_weight.shape[1] // 3
    local_blocks = shard_rows // BLK
    query = projected[:, :att_width].reshape(local_blocks, BLK, HEADS, HEAD_DIM)
    keys = projected[:, att_width : 2 * att_width]
    values = projected[:, 2 * att_width :]
    block_live = live_f.reshape(local_blocks, BLK)
    divisor = jnp.maximum(jnp.sum(block_live, axis=1), 1.0)[:, None]
    short_keys = (
        jnp.sum(
            keys.astype(jnp.float32).reshape(local_blocks, BLK, att_width) * block_live[:, :, None],
            axis=1,
        )
        / divisor
    ).astype(jnp.bfloat16)
    short_values = (
        jnp.sum(
            values.astype(jnp.float32).reshape(local_blocks, BLK, att_width)
            * block_live[:, :, None],
            axis=1,
        )
        / divisor
    ).astype(jnp.bfloat16)
    every_keys, every_values = (
        lax.all_gather(short_keys, "space", axis=0, tiled=True),
        lax.all_gather(short_values, "space", axis=0, tiled=True),
    )
    chosen = block_choice[0]
    picked_keys = every_keys[chosen].reshape(local_blocks, SEL, HEADS, HEAD_DIM)
    picked_values = every_values[chosen].reshape(local_blocks, SEL, HEADS, HEAD_DIM)
    mixed = attend(
        query,
        keys.reshape(local_blocks, BLK, HEADS, HEAD_DIM),
        values.reshape(local_blocks, BLK, HEADS, HEAD_DIM),
        live.reshape(local_blocks, BLK),
        picked_keys,
        picked_values,
    )
    attended = (mixed.reshape(shard_rows, att_width) * live_f[:, None]).astype(jnp.bfloat16)
    columns = attended
    projected_out = jnp.dot(
        columns,
        lax.all_gather(output_weight, "space", axis=0, tiled=True),
        preferred_element_type=jnp.float32,
    )
    layer = (hidden + projected_out).astype(jnp.bfloat16)[None]
    upstream = cotangent[0]
    factor = (lax.axis_size("dp") * space_count * shard_rows) ** (-0.5)
    shard_sum = lax.psum_scatter(
        jnp.dot(attended.T, upstream, preferred_element_type=jnp.float32).astype(jnp.bfloat16),
        "space",
        scatter_dimension=0,
        tiled=True,
    )
    gradient = lax.psum(shard_sum, "dp").astype(jnp.float32)
    return (layer, gradient * factor)


NEG = -1e30
F32 = jnp.float32
BF16 = jnp.bfloat16
ROWS_CONTRACT = (((0,), (0,)), ((), ()))
LANES_CONTRACT = (((1,), (1,)), ((), ()))


def vmem():
    return pl.BlockSpec(memory_space=pltpu.VMEM)


def smem():
    return pl.BlockSpec(memory_space=pltpu.SMEM)


def call(kernel, scalars, arrays, outs, scratch, name, flops):
    size = sum(a.size * a.dtype.itemsize for a in list(arrays) + list(outs))
    return pl.pallas_call(
        kernel,
        out_shape=tuple(outs),
        in_specs=[smem()] + [vmem()] * len(arrays),
        out_specs=tuple(vmem() for _ in outs),
        scratch_shapes=scratch,
        name=name,
        compiler_params=pltpu.CompilerParams(vmem_limit_bytes=24 * 1024 * 1024),
        cost_estimate=pl.CostEstimate(flops=flops, bytes_accessed=size, transcendentals=0),
    )(scalars, *arrays)


def pack_kernel(groups, width, scalars, feats, near, misc, weight, *packs):
    z = scalars[0]
    rows, cin = feats.shape
    depth = weight.shape[0]
    att = weight.shape[1] // 3
    taps = near.shape[0]
    tail = 3 * width - 2 * cin
    high = near[...] // 32
    low = near[...] - high * 32
    for pack in packs:
        pack[0:rows, :] = feats[...]
        start = rows + 2 * depth + depth * tail // cin
        info = jnp.concatenate([high, low], axis=1).astype(F32)
        info = jnp.concatenate([info, misc[...].astype(F32)], axis=0)
        pack[start : start + taps + 2, :] = info.astype(BF16)
    for group in range(groups):
        piece = jnp.concatenate(
            [weight[:, part * att + group * width : part * att + (group + 1) * width] for part in range(3)],
            axis=1,
        )
        for offset, pack in enumerate(packs):

            @pl.when((z ^ group) == offset)
            def _(pack=pack, piece=piece):
                pack[rows : rows + depth, :] = piece[:, 0:cin]
                pack[rows + depth : rows + 2 * depth, :] = piece[:, cin : 2 * cin]
                strip = depth * tail // cin
                for i in range(cin // tail):
                    pack[rows + 2 * depth : rows + 2 * depth + strip, i * tail : (i + 1) * tail] = piece[
                        i * strip : (i + 1) * strip, 2 * cin :
                    ]


def taps_kernel(groups, rows, cap, info, scalars, mine, other, out, every, table):
    z, c = scalars[0], scalars[1]
    slots = 2 * groups * cap
    for s in range(groups):
        every[s * rows : (s + 1) * rows, :] = mine[s, 0:rows, :]
        every[(groups + s) * rows : (groups + s + 1) * rows, :] = other[s, 0:rows, :]
    slot = lax.broadcasted_iota(jnp.int32, (1, slots), 1)
    peer = slot // cap
    base = (((peer // 2) ^ z) + groups * ((peer & 1) ^ c)) * rows
    place = lax.broadcasted_iota(jnp.int32, (2 * groups * rows, slots), 0)
    entry = lax.broadcasted_iota(jnp.int32, (table.shape[0], rows), 0)
    for s in range(groups):
        wanted = mine[s, info + 6 : info + 7, 0:slots].astype(F32).astype(jnp.int32) + base
        pick = jnp.where(place == wanted, 1.0, 0.0).astype(BF16)
        halo = lax.dot_general(pick, every[...], ROWS_CONTRACT, preferred_element_type=F32)
        table[0:rows, :] = mine[s, 0:rows, :]
        table[rows : rows + slots, :] = halo.astype(BF16)
        table[rows + slots :, :] = jnp.zeros((table.shape[0] - rows - slots, table.shape[1]), BF16)
        out[0, s * rows : (s + 1) * rows, :] = mine[s, 0:rows, :]
        for k in range(6):
            pair = mine[s, info + k : info + k + 1, :].astype(F32).astype(jnp.int32)
            index = pair[:, 0:rows] * 32 + pair[:, rows : 2 * rows]
            pick = jnp.where(entry == index, 1.0, 0.0).astype(BF16)
            row = lax.dot_general(pick, table[...], ROWS_CONTRACT, preferred_element_type=F32)
            out[k + 1, s * rows : (s + 1) * rows, :] = row.astype(BF16)


def conv_kernel(groups, parts, rows, scalars, taps, gain, *refs):
    z, c, d = scalars[0], scalars[1], scalars[2]
    own, own_other, near, near_other = refs[0:4]
    far = refs[4 : 4 + parts - 1]
    far_other = refs[4 + parts - 1 : 4 + 2 * (parts - 1)]
    mine, other = refs[4 + 2 * (parts - 1) : 6 + 2 * (parts - 1)]
    hidden_out, projected_out, summary_out, weight, proj, hidden, normed = refs[6 + 2 * (parts - 1) :]
    depth = own.shape[1]
    cut = near.shape[-1]
    pdepth = proj.shape[0] // (2 * groups)
    cin = mine.shape[2]
    width = projected_out.shape[1] // 3
    tail = 3 * width - 2 * cin
    strip = pdepth * tail // cin

    def at(row, size):
        return pl.ds(pl.multiple_of(row, size), size)

    for core, whole, piece, others in ((c, own, near, far), (1 - c, own_other, near_other, far_other)):
        weight[:, at((2 * z + core) * depth, depth), :] = whole[...]
        for k in range(1, groups):
            band = at((2 * (z ^ k) + core) * depth, depth)
            weight[:, band, at(d * cut, cut)] = piece[k - 1]
            for m in range(1, parts):
                weight[:, band, at((d ^ m) * cut, cut)] = others[m - 1][k - 1]
    for core, pack in ((c, mine), (1 - c, other)):
        for k in range(groups):
            first = (2 * (z ^ k) + core) * pdepth
            band = at(first, pdepth)
            proj[band, 0:cin] = pack[k, rows : rows + pdepth, :]
            proj[band, cin : 2 * cin] = pack[k, rows + pdepth : rows + 2 * pdepth, :]
            for i in range(cin // tail):
                proj[at(first + i * strip, strip), 2 * cin : 2 * cin + tail] = pack[
                    k, rows + 2 * pdepth : rows + 2 * pdepth + strip, i * tail : (i + 1) * tail
                ]
    count_taps = taps.shape[0]
    total = jnp.dot(taps[0], weight[0], preferred_element_type=F32)
    for k in range(1, count_taps):
        total = total + jnp.dot(taps[k], weight[k], preferred_element_type=F32)
    hidden[...] = total
    place = lax.broadcasted_iota(jnp.int32, (rows, 1), 0)
    for s in range(groups):
        band = slice(s * rows, (s + 1) * rows)
        h = jnp.where(place < scalars[3 + s], hidden[band, :], 0.0)
        if s == 0:
            hidden_out[...] = h
        power = jnp.mean(h * h, axis=-1, keepdims=True)
        normed[band, :] = (h * lax.rsqrt(power + 1e-06) * gain[...]).astype(BF16)
    projected_out[...] = jnp.dot(
        normed[...], proj[:, 0 : 3 * width], preferred_element_type=F32
    ).astype(BF16)
    blocks = groups * rows // BLK
    block = lax.broadcasted_iota(jnp.int32, (blocks, groups * rows), 0)
    token = lax.broadcasted_iota(jnp.int32, (blocks, groups * rows), 1)
    shard = lax.broadcasted_iota(jnp.int32, (blocks, 1), 0) // (rows // BLK)
    count = jnp.zeros((blocks, 1), jnp.int32)
    for s in range(groups):
        count = jnp.where(shard == s, scalars[3 + s], count)
    member = (token // BLK == block) & (token - shard * rows < count)
    member = jnp.where(member, 1.0, 0.0)
    divisor = jnp.maximum(jnp.sum(member, axis=1, keepdims=True), 1.0)
    sums = jnp.dot(
        member.astype(BF16), projected_out[:, width : 3 * width], preferred_element_type=F32
    )
    summary_out[...] = (sums / divisor).astype(BF16)


def attend_kernel(groups, heads, rows, scalars, projected, mine, other, bias, cotangent, own, own_other, hidden,
                  *refs):
    c = scalars[1]
    base_out, grad_out, send_out = refs[0:3]
    shares = refs[3 : 3 + groups - 1]
    attended, outw, grad = refs[3 + groups - 1 :]
    width = heads * HEAD_DIM
    half = own.shape[0]
    outw[pl.ds(pl.multiple_of(c * half, half), half), :] = own[...]
    outw[pl.ds(pl.multiple_of((1 - c) * half, half), half), :] = own_other[...]
    short = jnp.concatenate([mine[...].astype(F32), other[...].astype(F32)], axis=0).astype(BF16)
    scale = HEAD_DIM ** (-0.5)
    across = lax.broadcasted_iota(jnp.int32, (rows, rows), 1)
    down = lax.broadcasted_iota(jnp.int32, (rows, rows), 0)
    same = across // BLK == down // BLK
    place = lax.broadcasted_iota(jnp.int32, (rows, 1), 0)
    for s in range(groups):
        count = scalars[3 + s]
        band = slice(s * rows, (s + 1) * rows)
        open_keys = same & (across < count)
        live = place < count
        far_bias = jnp.concatenate(
            [
                jnp.broadcast_to(bias[s, b : b + 1, :], (BLK, bias.shape[2]))
                for b in range(rows // BLK)
            ],
            axis=0,
        )
        for h in range(heads):
            lane = slice(h * HEAD_DIM, (h + 1) * HEAD_DIM)
            query = projected[band, lane]
            key = projected[band, width + h * HEAD_DIM : width + (h + 1) * HEAD_DIM]
            value = projected[band, 2 * width + h * HEAD_DIM : 2 * width + (h + 1) * HEAD_DIM]
            near = lax.dot_general(query, key, LANES_CONTRACT, preferred_element_type=F32) * scale
            near = jnp.where(open_keys, near, NEG)
            far = lax.dot_general(query, short[:, lane], LANES_CONTRACT, preferred_element_type=F32)
            far = far * scale + far_bias
            highest = jnp.maximum(
                jnp.max(near, axis=-1, keepdims=True), jnp.max(far, axis=-1, keepdims=True)
            )
            near = jnp.exp(near - highest)
            far = jnp.exp(far - highest)
            total = jnp.sum(near, axis=-1, keepdims=True) + jnp.sum(far, axis=-1, keepdims=True)
            near = (near / total).astype(BF16)
            far = (far / total).astype(BF16)
            mixed = jnp.dot(near, value, preferred_element_type=F32) + jnp.dot(
                far, short[:, width + h * HEAD_DIM : width + (h + 1) * HEAD_DIM], preferred_element_type=F32
            )
            attended[band, lane] = jnp.where(live, mixed, 0.0).astype(BF16)
    for s in range(groups):
        share = jnp.dot(attended[s * rows : (s + 1) * rows, :], outw[...], preferred_element_type=F32)
        if s == 0:
            base_out[...] = hidden[...] + share
        else:
            shares[s - 1][...] = share.astype(BF16)
    total = lax.dot_general(attended[0:rows, :], cotangent[0], ROWS_CONTRACT, preferred_element_type=F32)
    for s in range(1, groups):
        total = total + lax.dot_general(
            attended[s * rows : (s + 1) * rows, :], cotangent[s], ROWS_CONTRACT, preferred_element_type=F32
        )
    grad[...] = total
    grad_out[...] = grad[pl.ds(pl.multiple_of(c * half, half), half), :]
    send_out[...] = grad[pl.ds(pl.multiple_of((1 - c) * half, half), half), :].astype(BF16)


def paired_shards(
    voxel_feats,
    neighbours,
    wanted_rows,
    live_counts,
    block_choice,
    conv_weight,
    norm_gain,
    input_weight,
    output_weight,
    cotangent,
):
    space = lax.axis_size("space")
    parts = lax.axis_size("dp")
    groups = space // 2
    position = lax.axis_index("space")
    d = lax.axis_index("dp")
    z, c = position // 2, position % 2
    rows, cin = voxel_feats.shape[1:]
    taps = neighbours.shape[2]
    cap = wanted_rows.shape[3]
    depth, out_width = conv_weight.shape[1:]
    pdepth = input_weight.shape[0]
    att = input_weight.shape[1] // 3
    width = att // groups
    heads = width // HEAD_DIM
    local_blocks = rows // BLK
    half = output_weight.shape[0]
    cut = out_width // parts

    def over_z(x, k):
        return lax.ppermute(x, "space", [(i, ((i // 2) ^ k) * 2 + i % 2) for i in range(space)])

    def over_core(x):
        return lax.ppermute(x, "space", [(i, i ^ 1) for i in range(space)])

    def over_dp(x, m):
        return lax.ppermute(x, "dp", [(i, i ^ m) for i in range(parts)])

    counts = live_counts[0]
    relative = jnp.arange(groups, dtype=jnp.int32) ^ z
    scalars = jnp.concatenate(
        [jnp.stack([z, c, d]).astype(jnp.int32), counts[2 * relative + c], jnp.zeros((1,), jnp.int32)]
    )

    quarter = lax.dynamic_slice_in_dim(conv_weight, d * cut, cut, axis=2)
    near = jnp.stack([over_z(quarter, k) for k in range(1, groups)])

    slots = space * cap
    misc = jnp.zeros((2, cin), jnp.int32)
    misc = misc.at[0, 0:slots].set(wanted_rows.reshape(slots))
    misc = misc.at[1, 0 : block_choice.shape[1] * SEL].set(block_choice.reshape(-1))
    info = rows + 2 * pdepth + pdepth * (3 * width - 2 * cin) // cin
    pack_rows = -(-(info + taps + 2) // 16) * 16
    packs = call(
        functools.partial(pack_kernel, groups, width),
        scalars,
        [voxel_feats[0], neighbours[0].T, misc, input_weight],
        [jax.ShapeDtypeStruct((pack_rows, cin), BF16)] * groups,
        [],
        "pack",
        1000,
    )
    mine = jnp.stack([packs[0]] + [over_z(packs[k], k) for k in range(1, groups)])

    own_other = over_core(conv_weight)
    out_other = over_core(output_weight)
    far = [over_dp(near, m) for m in range(1, parts)]
    near_other = over_core(near)
    other = over_core(mine)
    cots = jnp.stack([cotangent[0]] + [over_z(cotangent[0], k) for k in range(1, groups)])
    far_other = [over_core(x) for x in far]

    tokens = groups * rows
    table_rows = -(-(rows + slots + 1) // 128) * 128
    (gathered,) = call(
        functools.partial(taps_kernel, groups, rows, cap, info),
        scalars,
        [mine, other],
        [jax.ShapeDtypeStruct((taps + 1, tokens, cin), BF16)],
        [pltpu.VMEM((2 * tokens, cin), BF16), pltpu.VMEM((table_rows, cin), BF16)],
        "taps",
        2 * taps * tokens * table_rows * cin,
    )
    hidden, projected, summary = call(
        functools.partial(conv_kernel, groups, parts, rows),
        scalars,
        [gathered, norm_gain[None, :], conv_weight, own_other, near, near_other, *far, *far_other, mine, other],
        [
            jax.ShapeDtypeStruct((rows, out_width), F32),
            jax.ShapeDtypeStruct((tokens, 3 * width), BF16),
            jax.ShapeDtypeStruct((groups * local_blocks, 2 * width), BF16),
        ],
        [
            pltpu.VMEM((taps + 1, cin, out_width), BF16),
            pltpu.VMEM((space * pdepth, -(-3 * width // 128) * 128), BF16),
            pltpu.VMEM((tokens, out_width), F32),
            pltpu.VMEM((tokens, out_width), BF16),
        ],
        "conv",
        2 * tokens * out_width * ((taps + 1) * cin + 3 * width),
    )
    summary_other = over_core(summary)

    chosen = mine[:, info + taps + 1, 0 : local_blocks * SEL].astype(F32).astype(jnp.int32)
    chosen = chosen.reshape(groups, local_blocks, SEL)
    inner = jnp.arange(local_blocks, dtype=jnp.int32)
    named = jnp.concatenate(
        [((2 * relative + core)[:, None] * local_blocks + inner[None, :]).reshape(-1) for core in (c, 1 - c)]
    )
    bias = jnp.where(jnp.any(chosen[..., None] == named, axis=2), 0.0, NEG).astype(F32)

    outs = call(
        functools.partial(attend_kernel, groups, heads, rows),
        scalars,
        [projected, summary, summary_other, bias, cots, output_weight, out_other, hidden],
        [
            jax.ShapeDtypeStruct((rows, out_width), F32),
            jax.ShapeDtypeStruct((half, out_width), F32),
            jax.ShapeDtypeStruct((half, out_width), BF16),
        ]
        + [jax.ShapeDtypeStruct((rows, out_width), BF16)] * (groups - 1),
        [
            pltpu.VMEM((tokens, width), BF16),
            pltpu.VMEM((2 * half, out_width), BF16),
            pltpu.VMEM((2 * half, out_width), F32),
        ],
        "attend",
        8 * tokens * width * (rows + out_width),
    )
    base, grad, send = outs[0:3]
    received = [over_z(outs[2 + k], k) for k in range(1, groups)]
    grad = (grad + over_core(send).astype(F32)).astype(BF16)
    terms = [grad.astype(F32)] + [over_dp(grad, m).astype(F32) for m in range(1, parts)]
    while len(terms) > 1:
        terms = [terms[i] + terms[i + 1] for i in range(0, len(terms), 2)]
    factor = (parts * space * rows) ** (-0.5)
    layer = base
    for x in received:
        layer = layer + x.astype(F32)
    return (layer.astype(BF16)[None], terms[0] * factor)


def section(mesh, *args):
    space, parts = mesh.shape["space"], mesh.shape["dp"]
    groups = space // 2
    powers = space % 2 == 0 and groups & (groups - 1) == 0 and parts & (parts - 1) == 0
    cin = args[0].shape[2]
    width = args[7].shape[1] // 3 // max(groups, 1)
    tail = 3 * width - 2 * cin
    fits = (
        powers
        and HEADS % max(groups, 1) == 0
        and args[5].shape[2] % (128 * parts) == 0
        and 0 < tail <= 128
        and cin % tail == 0
        and (args[7].shape[0] * tail) % (16 * cin) == 0
        and args[0].shape[1] * 2 == cin
        and space * args[2].shape[3] <= cin
    )
    return (paired_shards if fits else general_shards)(*args)


def solution(mesh):
    placed = (
        P("dp", "space", None),
        P("dp", "space", None),
        P("dp", "space", None, None),
        P("dp", None),
        P("dp", "space", None),
        P(None, "space", None),
        P(),
        P("space", None),
        P("space", None),
        P("dp", "space", None),
    )
    return jax.shard_map(
        functools.partial(section, mesh),
        mesh=mesh,
        in_specs=placed,
        out_specs=(P("dp", "space", None), P("space", None)),
        check_vma=False,
    )
```

```python
import functools

import jax
import jax.numpy as jnp
from jax import lax
from jax.experimental import pallas as pl
from jax.experimental.pallas import tpu as pltpu
from jax.sharding import PartitionSpec as P


HEADS = 12
HEAD_DIM = 64
BLK = 64
SEL = 4


def attend(query, keys, values, key_live, short_keys, short_values):
    scale = HEAD_DIM ** (-0.5)
    near = jnp.einsum("bqhd,bkhd->bhqk", query, keys, preferred_element_type=jnp.float32) * scale
    near = jnp.where(key_live[:, None, None, :], near, -1e30)
    far = (
        jnp.einsum("bqhd,bshd->bhqs", query, short_keys, preferred_element_type=jnp.float32) * scale
    )
    scores = jnp.concatenate([near, far], axis=-1)
    highest = jnp.max(scores, axis=-1, keepdims=True)
    weights = jnp.exp(scores - highest)
    weights = (weights / jnp.sum(weights, axis=-1, keepdims=True)).astype(jnp.bfloat16)
    mixed = jnp.einsum(
        "bhqk,bkhd->bqhd", weights[..., :BLK], values, preferred_element_type=jnp.float32
    )
    return mixed + jnp.einsum(
        "bhqs,bshd->bqhd", weights[..., BLK:], short_values, preferred_element_type=jnp.float32
    )


def general_shards(
    voxel_feats,
    neighbours,
    wanted_rows,
    live_counts,
    block_choice,
    conv_weight,
    norm_gain,
    input_weight,
    output_weight,
    cotangent,
):
    space_count = lax.axis_size("space")
    position = lax.axis_index("space")
    own_rows = voxel_feats[0]
    shard_rows = own_rows.shape[0]
    index_map = neighbours[0]
    zero_row = jnp.zeros((1, own_rows.shape[1]), jnp.bfloat16)
    requested = lax.all_to_all(wanted_rows[0, 0], "space", split_axis=0, concat_axis=0, tiled=True)
    answers = own_rows[requested]
    arrived = lax.all_to_all(answers, "space", split_axis=0, concat_axis=0, tiled=True)
    padded = jnp.concatenate([own_rows, arrived.reshape(-1, own_rows.shape[1]), zero_row], axis=0)
    gathered_taps = padded[index_map]
    table = jnp.concatenate([own_rows[:, None, :], gathered_taps], axis=1)
    columns = table
    hidden = jnp.einsum(
        "tkr,kro->to",
        columns,
        lax.all_gather(conv_weight, "space", axis=1, tiled=True),
        preferred_element_type=jnp.float32,
    )
    live_count = lax.dynamic_index_in_dim(live_counts[0], position, keepdims=False)
    live = jnp.arange(shard_rows, dtype=jnp.int32) < live_count
    live_f = live.astype(jnp.float32)
    hidden = hidden * live_f[:, None]
    power = jnp.mean(hidden * hidden, axis=-1, keepdims=True)
    normed = (hidden * lax.rsqrt(power + 1e-06) * norm_gain).astype(jnp.bfloat16)
    columns = normed
    projected = jnp.dot(
        columns,
        lax.all_gather(input_weight, "space", axis=0, tiled=True),
        preferred_element_type=jnp.float32,
    ).astype(jnp.bfloat16)
    att_width = input_weight.shape[1] // 3
    local_blocks = shard_rows // BLK
    query = projected[:, :att_width].reshape(local_blocks, BLK, HEADS, HEAD_DIM)
    keys = projected[:, att_width : 2 * att_width]
    values = projected[:, 2 * att_width :]
    block_live = live_f.reshape(local_blocks, BLK)
    divisor = jnp.maximum(jnp.sum(block_live, axis=1), 1.0)[:, None]
    short_keys = (
        jnp.sum(
            keys.astype(jnp.float32).reshape(local_blocks, BLK, att_width) * block_live[:, :, None],
            axis=1,
        )
        / divisor
    ).astype(jnp.bfloat16)
    short_values = (
        jnp.sum(
            values.astype(jnp.float32).reshape(local_blocks, BLK, att_width)
            * block_live[:, :, None],
            axis=1,
        )
        / divisor
    ).astype(jnp.bfloat16)
    every_keys, every_values = (
        lax.all_gather(short_keys, "space", axis=0, tiled=True),
        lax.all_gather(short_values, "space", axis=0, tiled=True),
    )
    chosen = block_choice[0]
    picked_keys = every_keys[chosen].reshape(local_blocks, SEL, HEADS, HEAD_DIM)
    picked_values = every_values[chosen].reshape(local_blocks, SEL, HEADS, HEAD_DIM)
    mixed = attend(
        query,
        keys.reshape(local_blocks, BLK, HEADS, HEAD_DIM),
        values.reshape(local_blocks, BLK, HEADS, HEAD_DIM),
        live.reshape(local_blocks, BLK),
        picked_keys,
        picked_values,
    )
    attended = (mixed.reshape(shard_rows, att_width) * live_f[:, None]).astype(jnp.bfloat16)
    columns = attended
    projected_out = jnp.dot(
        columns,
        lax.all_gather(output_weight, "space", axis=0, tiled=True),
        preferred_element_type=jnp.float32,
    )
    layer = (hidden + projected_out).astype(jnp.bfloat16)[None]
    upstream = cotangent[0]
    factor = (lax.axis_size("dp") * space_count * shard_rows) ** (-0.5)
    shard_sum = lax.psum_scatter(
        jnp.dot(attended.T, upstream, preferred_element_type=jnp.float32).astype(jnp.bfloat16),
        "space",
        scatter_dimension=0,
        tiled=True,
    )
    gradient = lax.psum(shard_sum, "dp").astype(jnp.float32)
    return (layer, gradient * factor)


NEG = -1e30
F32 = jnp.float32
BF16 = jnp.bfloat16
ROWS_CONTRACT = (((0,), (0,)), ((), ()))
LANES_CONTRACT = (((1,), (1,)), ((), ()))


def vmem():
    return pl.BlockSpec(memory_space=pltpu.VMEM)


def smem():
    return pl.BlockSpec(memory_space=pltpu.SMEM)


def call(kernel, scalars, arrays, outs, scratch, flops):
    size = sum(a.size * a.dtype.itemsize for a in list(arrays) + list(outs))
    return pl.pallas_call(
        kernel,
        out_shape=tuple(outs),
        in_specs=[smem()] * len(scalars) + [vmem()] * len(arrays),
        out_specs=tuple(vmem() for _ in outs),
        scratch_shapes=scratch,
        compiler_params=pltpu.CompilerParams(vmem_limit_bytes=24 * 1024 * 1024),
        cost_estimate=pl.CostEstimate(flops=flops, bytes_accessed=size, transcendentals=0),
    )(*scalars, *arrays)


def pack_kernel(groups, width, scalars, feats, near, wanted, chosen, weight, *refs):
    packs, info = refs[:groups], refs[groups]
    z = scalars[0]
    rows, cin = feats.shape
    depth = weight.shape[0]
    att = weight.shape[1] // 3
    taps = near.shape[0]
    tail = 3 * width - 2 * cin
    strip = depth * tail // cin
    info[...] = jnp.zeros_like(info)
    for k in range(taps):
        high = near[k] // 32
        info[k : k + 1, 0:rows] = high.astype(F32)
        info[k : k + 1, rows : 2 * rows] = (near[k] - high * 32).astype(F32)
    cap = wanted.shape[1]
    for p in range(wanted.shape[0]):
        info[taps : taps + 1, p * cap : (p + 1) * cap] = wanted[p : p + 1, :].astype(F32)
    for b in range(chosen.shape[0]):
        info[taps + 1 : taps + 2, b * SEL : (b + 1) * SEL] = chosen[b : b + 1, :].astype(F32)
    start = rows + 2 * depth + strip
    for pack in packs:
        pack[0:rows, :] = feats[...]
        pack[start : start + info.shape[0], :] = info[...].astype(BF16)
    for group in range(groups):
        piece = jnp.concatenate(
            [weight[:, part * att + group * width : part * att + (group + 1) * width] for part in range(3)],
            axis=1,
        )
        for offset, pack in enumerate(packs):

            @pl.when((z ^ group) == offset)
            def _(pack=pack, piece=piece):
                pack[rows : rows + depth, :] = piece[:, 0:cin]
                pack[rows + depth : rows + 2 * depth, :] = piece[:, cin : 2 * cin]
                for i in range(cin // tail):
                    pack[rows + 2 * depth : rows + 2 * depth + strip, i * tail : (i + 1) * tail] = piece[
                        i * strip : (i + 1) * strip, 2 * cin :
                    ]


def taps_kernel(groups, rows, cap, info, scalars, mine, other, out, every, table):
    z, c = scalars[0], scalars[1]
    slots = 2 * groups * cap
    for s in range(groups):
        every[s * rows : (s + 1) * rows, :] = mine[s, 0:rows, :]
        every[(groups + s) * rows : (groups + s + 1) * rows, :] = other[s, 0:rows, :]
    slot = lax.broadcasted_iota(jnp.int32, (1, slots), 1)
    peer = slot // cap
    base = (((peer // 2) ^ z) + groups * ((peer & 1) ^ c)) * rows
    place = lax.broadcasted_iota(jnp.int32, (2 * groups * rows, slots), 0)
    entry = lax.broadcasted_iota(jnp.int32, (table.shape[0], rows), 0)
    for s in range(groups):
        wanted = mine[s, info + 6 : info + 7, 0:slots].astype(F32).astype(jnp.int32) + base
        pick = jnp.where(place == wanted, 1.0, 0.0).astype(BF16)
        halo = lax.dot_general(pick, every[...], ROWS_CONTRACT, preferred_element_type=F32)
        table[0:rows, :] = mine[s, 0:rows, :]
        table[rows : rows + slots, :] = halo.astype(BF16)
        table[rows + slots :, :] = jnp.zeros((table.shape[0] - rows - slots, table.shape[1]), BF16)
        out[0, s * rows : (s + 1) * rows, :] = mine[s, 0:rows, :]
        for k in range(6):
            pair = mine[s, info + k : info + k + 1, :].astype(F32).astype(jnp.int32)
            index = pair[:, 0:rows] * 32 + pair[:, rows : 2 * rows]
            pick = jnp.where(entry == index, 1.0, 0.0).astype(BF16)
            row = lax.dot_general(pick, table[...], ROWS_CONTRACT, preferred_element_type=F32)
            out[k + 1, s * rows : (s + 1) * rows, :] = row.astype(BF16)


def conv_kernel(groups, parts, rows, scalars, counts, taps, gain, *refs):
    z, c, d = scalars[0], scalars[1], scalars[2]
    live = [counts[0, 2 * (z ^ s) + c] for s in range(groups)]
    own, own_other, near, near_other = refs[0:4]
    far = refs[4 : 4 + parts - 1]
    far_other = refs[4 + parts - 1 : 4 + 2 * (parts - 1)]
    mine, other = refs[4 + 2 * (parts - 1) : 6 + 2 * (parts - 1)]
    hidden_out, projected_out, summary_out, weight, proj, hidden, normed = refs[6 + 2 * (parts - 1) :]
    depth = own.shape[1]
    cut = near.shape[-1]
    pdepth = proj.shape[0] // (2 * groups)
    cin = mine.shape[2]
    width = projected_out.shape[1] // 3
    tail = 3 * width - 2 * cin
    strip = pdepth * tail // cin

    def at(row, size):
        return pl.ds(pl.multiple_of(row, size), size)

    for core, whole, piece, others in ((c, own, near, far), (1 - c, own_other, near_other, far_other)):
        weight[:, at((2 * z + core) * depth, depth), :] = whole[...]
        for k in range(1, groups):
            band = at((2 * (z ^ k) + core) * depth, depth)
            weight[:, band, at(d * cut, cut)] = piece[k - 1]
            for m in range(1, parts):
                weight[:, band, at((d ^ m) * cut, cut)] = others[m - 1][k - 1]
    for core, pack in ((c, mine), (1 - c, other)):
        for k in range(groups):
            first = (2 * (z ^ k) + core) * pdepth
            band = at(first, pdepth)
            proj[band, 0:cin] = pack[k, rows : rows + pdepth, :]
            proj[band, cin : 2 * cin] = pack[k, rows + pdepth : rows + 2 * pdepth, :]
            for i in range(cin // tail):
                proj[at(first + i * strip, strip), 2 * cin : 2 * cin + tail] = pack[
                    k, rows + 2 * pdepth : rows + 2 * pdepth + strip, i * tail : (i + 1) * tail
                ]
    count_taps = taps.shape[0]
    total = jnp.dot(taps[0], weight[0], preferred_element_type=F32)
    for k in range(1, count_taps):
        total = total + jnp.dot(taps[k], weight[k], preferred_element_type=F32)
    hidden[...] = total
    place = lax.broadcasted_iota(jnp.int32, (rows, 1), 0)
    for s in range(groups):
        band = slice(s * rows, (s + 1) * rows)
        h = jnp.where(place < live[s], hidden[band, :], 0.0)
        if s == 0:
            hidden_out[...] = h
        power = jnp.mean(h * h, axis=-1, keepdims=True)
        normed[band, :] = (h * lax.rsqrt(power + 1e-06) * gain[...]).astype(BF16)
    projected_out[...] = jnp.dot(
        normed[...], proj[:, 0 : 3 * width], preferred_element_type=F32
    ).astype(BF16)
    blocks = groups * rows // BLK
    block = lax.broadcasted_iota(jnp.int32, (blocks, groups * rows), 0)
    token = lax.broadcasted_iota(jnp.int32, (blocks, groups * rows), 1)
    shard = lax.broadcasted_iota(jnp.int32, (blocks, 1), 0) // (rows // BLK)
    count = jnp.zeros((blocks, 1), jnp.int32)
    for s in range(groups):
        count = jnp.where(shard == s, live[s], count)
    member = (token // BLK == block) & (token - shard * rows < count)
    member = jnp.where(member, 1.0, 0.0)
    divisor = jnp.maximum(jnp.sum(member, axis=1, keepdims=True), 1.0)
    sums = jnp.dot(
        member.astype(BF16), projected_out[:, width : 3 * width], preferred_element_type=F32
    )
    summary_out[...] = (sums / divisor).astype(BF16)


def attend_kernel(groups, heads, rows, info, scalars, counts, projected, mine, other, packed, cotangent, own, own_other, hidden,
                  *refs):
    z, c = scalars[0], scalars[1]
    base_out, grad_out, send_out = refs[0:3]
    shares = refs[3 : 3 + groups - 1]
    attended, outw, grad = refs[3 + groups - 1 :]
    width = heads * HEAD_DIM
    half = own.shape[0]
    outw[pl.ds(pl.multiple_of(c * half, half), half), :] = own[...]
    outw[pl.ds(pl.multiple_of((1 - c) * half, half), half), :] = own_other[...]
    short = jnp.concatenate([mine[...].astype(F32), other[...].astype(F32)], axis=0).astype(BF16)
    scale = HEAD_DIM ** (-0.5)
    across = lax.broadcasted_iota(jnp.int32, (rows, rows), 1)
    down = lax.broadcasted_iota(jnp.int32, (rows, rows), 0)
    same = across // BLK == down // BLK
    place = lax.broadcasted_iota(jnp.int32, (rows, 1), 0)
    local_blocks = rows // BLK
    picks = (local_blocks * SEL, 128)
    diagonal = lax.broadcasted_iota(jnp.int32, picks, 0) == lax.broadcasted_iota(jnp.int32, picks, 1)
    slot = lax.broadcasted_iota(jnp.int32, (1, short.shape[0]), 1)
    shard = slot // local_blocks
    core = jnp.where(shard < groups, c, 1 - c)
    named = (2 * ((shard % groups) ^ z) + core) * local_blocks + slot % local_blocks
    for s in range(groups):
        count = counts[0, 2 * (z ^ s) + c]
        band = slice(s * rows, (s + 1) * rows)
        open_keys = same & (across < count)
        live = place < count
        entries = packed[s, info : info + 1, 0:128].astype(F32)
        entries = jnp.sum(jnp.where(diagonal, entries, 0.0), axis=1, keepdims=True)
        hits = jnp.where(entries.astype(jnp.int32) == named, 0.0, NEG)
        far_bias = jnp.concatenate(
            [
                jnp.broadcast_to(
                    jnp.max(hits[b * SEL : (b + 1) * SEL, :], axis=0, keepdims=True), (BLK, named.shape[1])
                )
                for b in range(local_blocks)
            ],
            axis=0,
        )
        for h in range(heads):
            lane = slice(h * HEAD_DIM, (h + 1) * HEAD_DIM)
            query = projected[band, lane]
            key = projected[band, width + h * HEAD_DIM : width + (h + 1) * HEAD_DIM]
            value = projected[band, 2 * width + h * HEAD_DIM : 2 * width + (h + 1) * HEAD_DIM]
            near = lax.dot_general(query, key, LANES_CONTRACT, preferred_element_type=F32) * scale
            near = jnp.where(open_keys, near, NEG)
            far = lax.dot_general(query, short[:, lane], LANES_CONTRACT, preferred_element_type=F32)
            far = far * scale + far_bias
            highest = jnp.maximum(
                jnp.max(near, axis=-1, keepdims=True), jnp.max(far, axis=-1, keepdims=True)
            )
            near = jnp.exp(near - highest)
            far = jnp.exp(far - highest)
            total = jnp.sum(near, axis=-1, keepdims=True) + jnp.sum(far, axis=-1, keepdims=True)
            near = (near / total).astype(BF16)
            far = (far / total).astype(BF16)
            mixed = jnp.dot(near, value, preferred_element_type=F32) + jnp.dot(
                far, short[:, width + h * HEAD_DIM : width + (h + 1) * HEAD_DIM], preferred_element_type=F32
            )
            attended[band, lane] = jnp.where(live, mixed, 0.0).astype(BF16)
    for s in range(groups):
        share = jnp.dot(attended[s * rows : (s + 1) * rows, :], outw[...], preferred_element_type=F32)
        if s == 0:
            base_out[...] = hidden[...] + share
        else:
            shares[s - 1][...] = share.astype(BF16)
    total = lax.dot_general(attended[0:rows, :], cotangent[0], ROWS_CONTRACT, preferred_element_type=F32)
    for s in range(1, groups):
        total = total + lax.dot_general(
            attended[s * rows : (s + 1) * rows, :], cotangent[s], ROWS_CONTRACT, preferred_element_type=F32
        )
    grad[...] = total
    grad_out[...] = grad[pl.ds(pl.multiple_of(c * half, half), half), :]
    send_out[...] = grad[pl.ds(pl.multiple_of((1 - c) * half, half), half), :].astype(BF16)


def paired_shards(
    voxel_feats,
    neighbours,
    wanted_rows,
    live_counts,
    block_choice,
    conv_weight,
    norm_gain,
    input_weight,
    output_weight,
    cotangent,
):
    space = lax.axis_size("space")
    parts = lax.axis_size("dp")
    groups = space // 2
    position = lax.axis_index("space")
    d = lax.axis_index("dp")
    z, c = position // 2, position % 2
    rows, cin = voxel_feats.shape[1:]
    taps = neighbours.shape[2]
    cap = wanted_rows.shape[3]
    _, out_width = conv_weight.shape[1:]
    pdepth = input_weight.shape[0]
    att = input_weight.shape[1] // 3
    width = att // groups
    heads = width // HEAD_DIM
    local_blocks = rows // BLK
    half = output_weight.shape[0]
    cut = out_width // parts

    def over_z(x, k):
        return lax.ppermute(x, "space", [(i, ((i // 2) ^ k) * 2 + i % 2) for i in range(space)])

    def over_core(x):
        return lax.ppermute(x, "space", [(i, i ^ 1) for i in range(space)])

    def over_dp(x, m):
        return lax.ppermute(x, "dp", [(i, i ^ m) for i in range(parts)])

    where = jnp.stack([z, c, d]).astype(jnp.int32)
    quarter = lax.dynamic_slice_in_dim(conv_weight, d * cut, cut, axis=2)
    near = jnp.stack([over_z(quarter, k) for k in range(1, groups)])

    slots = space * cap
    info = rows + 2 * pdepth + pdepth * (3 * width - 2 * cin) // cin
    info_rows = -(-(taps + 2) // 16) * 16
    packs = call(
        functools.partial(pack_kernel, groups, width),
        [where],
        [voxel_feats[0], neighbours.transpose(2, 0, 1), wanted_rows[0, 0], block_choice[0], input_weight],
        [jax.ShapeDtypeStruct((info + info_rows, cin), BF16)] * groups,
        [pltpu.VMEM((info_rows, cin), F32)],
        1000,
    )
    mine = jnp.stack([packs[0]] + [over_z(packs[k], k) for k in range(1, groups)])

    own_other = over_core(conv_weight)
    out_other = over_core(output_weight)
    far = [over_dp(near, m) for m in range(1, parts)]
    near_other = over_core(near)
    other = over_core(mine)
    cots = jnp.stack([cotangent[0]] + [over_z(cotangent[0], k) for k in range(1, groups)])
    far_other = [over_core(x) for x in far]

    tokens = groups * rows
    table_rows = -(-(rows + slots + 1) // 128) * 128
    (gathered,) = call(
        functools.partial(taps_kernel, groups, rows, cap, info),
        [where],
        [mine, other],
        [jax.ShapeDtypeStruct((taps + 1, tokens, cin), BF16)],
        [pltpu.VMEM((2 * tokens, cin), BF16), pltpu.VMEM((table_rows, cin), BF16)],
        2 * taps * tokens * table_rows * cin,
    )
    hidden, projected, summary = call(
        functools.partial(conv_kernel, groups, parts, rows),
        [where, live_counts],
        [gathered, norm_gain[None, :], conv_weight, own_other, near, near_other, *far, *far_other, mine, other],
        [
            jax.ShapeDtypeStruct((rows, out_width), F32),
            jax.ShapeDtypeStruct((tokens, 3 * width), BF16),
            jax.ShapeDtypeStruct((groups * local_blocks, 2 * width), BF16),
        ],
        [
            pltpu.VMEM((taps + 1, cin, out_width), BF16),
            pltpu.VMEM((space * pdepth, -(-3 * width // 128) * 128), BF16),
            pltpu.VMEM((tokens, out_width), F32),
            pltpu.VMEM((tokens, out_width), BF16),
        ],
        2 * tokens * out_width * ((taps + 1) * cin + 3 * width),
    )
    summary_other = over_core(summary)

    outs = call(
        functools.partial(attend_kernel, groups, heads, rows, info + taps + 1),
        [where, live_counts],
        [projected, summary, summary_other, mine, cots, output_weight, out_other, hidden],
        [
            jax.ShapeDtypeStruct((rows, out_width), F32),
            jax.ShapeDtypeStruct((half, out_width), F32),
            jax.ShapeDtypeStruct((half, out_width), BF16),
        ]
        + [jax.ShapeDtypeStruct((rows, out_width), BF16)] * (groups - 1),
        [
            pltpu.VMEM((tokens, width), BF16),
            pltpu.VMEM((2 * half, out_width), BF16),
            pltpu.VMEM((2 * half, out_width), F32),
        ],
        8 * tokens * width * (rows + out_width),
    )
    base, grad, send = outs[0:3]
    received = [over_z(outs[2 + k], k) for k in range(1, groups)]
    grad = (grad + over_core(send).astype(F32)).astype(BF16)
    terms = [grad.astype(F32)] + [over_dp(grad, m).astype(F32) for m in range(1, parts)]
    while len(terms) > 1:
        terms = [terms[i] + terms[i + 1] for i in range(0, len(terms), 2)]
    factor = (parts * space * rows) ** (-0.5)
    layer = base
    for x in received:
        layer = layer + x.astype(F32)
    return (layer.astype(BF16)[None], terms[0] * factor)


def section(mesh, *args):
    space, parts = mesh.shape["space"], mesh.shape["dp"]
    groups = space // 2
    powers = space % 2 == 0 and groups & (groups - 1) == 0 and parts & (parts - 1) == 0
    cin = args[0].shape[2]
    width = args[7].shape[1] // 3 // max(groups, 1)
    tail = 3 * width - 2 * cin
    fits = (
        powers
        and HEADS % max(groups, 1) == 0
        and args[5].shape[2] % (128 * parts) == 0
        and 0 < tail <= 128
        and cin % tail == 0
        and (args[7].shape[0] * tail) % (16 * cin) == 0
        and args[0].shape[1] * 2 == cin
        and space * args[2].shape[3] <= cin
    )
    if not fits:
        return general_shards(*args)
    return paired_shards(*args)


def solution(mesh):
    placed = (
        P("dp", "space", None),
        P("dp", "space", None),
        P("dp", "space", None, None),
        P("dp", None),
        P("dp", "space", None),
        P(None, "space", None),
        P(),
        P("space", None),
        P("space", None),
        P("dp", "space", None),
    )
    return jax.shard_map(
        functools.partial(section, mesh),
        mesh=mesh,
        in_specs=placed,
        out_specs=(P("dp", "space", None), P("space", None)),
        check_vma=False,
    )
```

```python
import functools

import jax
import jax.numpy as jnp
from jax import lax
from jax.experimental import pallas as pl
from jax.experimental.pallas import tpu as pltpu
from jax.sharding import PartitionSpec as P


HEADS = 12
HEAD_DIM = 64
BLK = 64
SEL = 4


def attend(query, keys, values, key_live, short_keys, short_values):
    scale = HEAD_DIM ** (-0.5)
    near = jnp.einsum("bqhd,bkhd->bhqk", query, keys, preferred_element_type=jnp.float32) * scale
    near = jnp.where(key_live[:, None, None, :], near, -1e30)
    far = (
        jnp.einsum("bqhd,bshd->bhqs", query, short_keys, preferred_element_type=jnp.float32) * scale
    )
    scores = jnp.concatenate([near, far], axis=-1)
    highest = jnp.max(scores, axis=-1, keepdims=True)
    weights = jnp.exp(scores - highest)
    weights = (weights / jnp.sum(weights, axis=-1, keepdims=True)).astype(jnp.bfloat16)
    mixed = jnp.einsum(
        "bhqk,bkhd->bqhd", weights[..., :BLK], values, preferred_element_type=jnp.float32
    )
    return mixed + jnp.einsum(
        "bhqs,bshd->bqhd", weights[..., BLK:], short_values, preferred_element_type=jnp.float32
    )


def general_shards(
    voxel_feats,
    neighbours,
    wanted_rows,
    live_counts,
    block_choice,
    conv_weight,
    norm_gain,
    input_weight,
    output_weight,
    cotangent,
):
    space_count = lax.axis_size("space")
    position = lax.axis_index("space")
    own_rows = voxel_feats[0]
    shard_rows = own_rows.shape[0]
    index_map = neighbours[0]
    zero_row = jnp.zeros((1, own_rows.shape[1]), jnp.bfloat16)
    requested = lax.all_to_all(wanted_rows[0, 0], "space", split_axis=0, concat_axis=0, tiled=True)
    answers = own_rows[requested]
    arrived = lax.all_to_all(answers, "space", split_axis=0, concat_axis=0, tiled=True)
    padded = jnp.concatenate([own_rows, arrived.reshape(-1, own_rows.shape[1]), zero_row], axis=0)
    gathered_taps = padded[index_map]
    table = jnp.concatenate([own_rows[:, None, :], gathered_taps], axis=1)
    columns = table
    hidden = jnp.einsum(
        "tkr,kro->to",
        columns,
        lax.all_gather(conv_weight, "space", axis=1, tiled=True),
        preferred_element_type=jnp.float32,
    )
    live_count = lax.dynamic_index_in_dim(live_counts[0], position, keepdims=False)
    live = jnp.arange(shard_rows, dtype=jnp.int32) < live_count
    live_f = live.astype(jnp.float32)
    hidden = hidden * live_f[:, None]
    power = jnp.mean(hidden * hidden, axis=-1, keepdims=True)
    normed = (hidden * lax.rsqrt(power + 1e-06) * norm_gain).astype(jnp.bfloat16)
    columns = normed
    projected = jnp.dot(
        columns,
        lax.all_gather(input_weight, "space", axis=0, tiled=True),
        preferred_element_type=jnp.float32,
    ).astype(jnp.bfloat16)
    att_width = input_weight.shape[1] // 3
    local_blocks = shard_rows // BLK
    query = projected[:, :att_width].reshape(local_blocks, BLK, HEADS, HEAD_DIM)
    keys = projected[:, att_width : 2 * att_width]
    values = projected[:, 2 * att_width :]
    block_live = live_f.reshape(local_blocks, BLK)
    divisor = jnp.maximum(jnp.sum(block_live, axis=1), 1.0)[:, None]
    short_keys = (
        jnp.sum(
            keys.astype(jnp.float32).reshape(local_blocks, BLK, att_width) * block_live[:, :, None],
            axis=1,
        )
        / divisor
    ).astype(jnp.bfloat16)
    short_values = (
        jnp.sum(
            values.astype(jnp.float32).reshape(local_blocks, BLK, att_width)
            * block_live[:, :, None],
            axis=1,
        )
        / divisor
    ).astype(jnp.bfloat16)
    every_keys, every_values = (
        lax.all_gather(short_keys, "space", axis=0, tiled=True),
        lax.all_gather(short_values, "space", axis=0, tiled=True),
    )
    chosen = block_choice[0]
    picked_keys = every_keys[chosen].reshape(local_blocks, SEL, HEADS, HEAD_DIM)
    picked_values = every_values[chosen].reshape(local_blocks, SEL, HEADS, HEAD_DIM)
    mixed = attend(
        query,
        keys.reshape(local_blocks, BLK, HEADS, HEAD_DIM),
        values.reshape(local_blocks, BLK, HEADS, HEAD_DIM),
        live.reshape(local_blocks, BLK),
        picked_keys,
        picked_values,
    )
    attended = (mixed.reshape(shard_rows, att_width) * live_f[:, None]).astype(jnp.bfloat16)
    columns = attended
    projected_out = jnp.dot(
        columns,
        lax.all_gather(output_weight, "space", axis=0, tiled=True),
        preferred_element_type=jnp.float32,
    )
    layer = (hidden + projected_out).astype(jnp.bfloat16)[None]
    upstream = cotangent[0]
    factor = (lax.axis_size("dp") * space_count * shard_rows) ** (-0.5)
    shard_sum = lax.psum_scatter(
        jnp.dot(attended.T, upstream, preferred_element_type=jnp.float32).astype(jnp.bfloat16),
        "space",
        scatter_dimension=0,
        tiled=True,
    )
    gradient = lax.psum(shard_sum, "dp").astype(jnp.float32)
    return (layer, gradient * factor)


NEG = -1e30
F32 = jnp.float32
PACK_LIMIT = 24000000
BF16 = jnp.bfloat16
ROWS_CONTRACT = (((0,), (0,)), ((), ()))
LANES_CONTRACT = (((1,), (1,)), ((), ()))


def spot():
    position = lax.axis_index("space")
    return position // 2, position % 2, lax.axis_index("dp")


def vmem():
    return pl.BlockSpec(memory_space=pltpu.VMEM)


def smem():
    return pl.BlockSpec(memory_space=pltpu.SMEM)


def call(kernel, scalars, arrays, outs, scratch, flops, space=pltpu.VMEM, limit=24 * 2**20):
    size = sum(a.size * a.dtype.itemsize for a in list(arrays) + list(outs))
    return pl.pallas_call(
        kernel,
        out_shape=tuple(outs),
        in_specs=[smem()] * len(scalars) + [pl.BlockSpec(memory_space=space)] * len(arrays),
        out_specs=tuple(vmem() for _ in outs),
        scratch_shapes=scratch,
        compiler_params=pltpu.CompilerParams(vmem_limit_bytes=limit),
        cost_estimate=pl.CostEstimate(flops=flops, bytes_accessed=size, transcendentals=0),
    )(*scalars, *([pltpu.with_memory_space_constraint(x, space) for x in arrays] if space == pltpu.HBM else arrays))


def pack_kernel(groups, width, rows, feats_in, near_in, wanted_in, chosen_in, weight_in, conv_in, *refs):
    voxels, own, beside = refs[0:3]
    quarters = refs[3 : groups + 1]
    near, wanted, chosen, weight, conv, pieces, info, sems = refs[groups + 1 :]
    z, _, d = spot()
    copies = [
        pltpu.make_async_copy(source, target, sems.at[i])
        for i, (source, target) in enumerate(
            (
                (weight_in, weight),
                (conv_in, conv),
                (feats_in, voxels.at[pl.ds(0, rows)]),
                (near_in, near),
                (wanted_in, wanted),
                (chosen_in, chosen),
            )
        )
    ]
    for copy in copies:
        copy.start()
    info[...] = jnp.zeros_like(info)
    copies[0].wait()
    depth = weight.shape[0]
    att = weight.shape[1] // 3
    taps, cdepth, out_width = conv.shape
    cut = quarters[0].shape[1]
    strip = depth * cut // out_width
    tail = 3 * width - out_width
    blank = jnp.zeros((depth, cut - tail), BF16)
    for group in range(groups):
        parts = [weight[:, p * att + group * width : p * att + (group + 1) * width] for p in range(3)]
        piece = jnp.concatenate(parts + [blank], axis=1)
        pieces[z ^ group, 0:depth, :] = piece[:, 0:out_width]
        for i in range(depth // strip):
            pieces[z ^ group, depth : depth + strip, i * cut : (i + 1) * cut] = piece[
                i * strip : (i + 1) * strip, out_width:
            ]
    lanes = pl.ds(pl.multiple_of(d * cut, cut), cut)
    copies[1].wait()
    for k in range(taps):
        band = slice(k * cdepth, (k + 1) * cdepth)
        own[band, :] = conv[k]
        beside[band, :] = conv[k]
        mine = conv[k, :, lanes]
        for quarter in quarters:
            quarter[band, :] = mine
    own[taps * cdepth :, :] = pieces[0]
    beside[taps * cdepth :, :] = pieces[1]
    for i, quarter in enumerate(quarters):
        quarter[taps * cdepth :, :] = pieces[2 + i, :, lanes]
    for copy in copies[2:]:
        copy.wait()
    for k in range(near.shape[0]):
        high = near[k] // 32
        info[k : k + 1, 0:rows] = high.astype(F32)
        info[k : k + 1, rows : 2 * rows] = (near[k] - high * 32).astype(F32)
    count = near.shape[0]
    cap = wanted.shape[1]
    for p in range(wanted.shape[0]):
        info[count : count + 1, p * cap : (p + 1) * cap] = wanted[p : p + 1, :].astype(F32)
    for b in range(chosen.shape[0]):
        info[count + 1 : count + 2, b * SEL : (b + 1) * SEL] = chosen[b : b + 1, :].astype(F32)
    voxels[rows:, :] = info[...].astype(BF16)


def taps_kernel(groups, rows, cap, info, mine, other, out, every, table):
    z, c, _ = spot()
    slots = 2 * groups * cap
    for s in range(groups):
        every[s * rows : (s + 1) * rows, :] = mine[s, 0:rows, :]
        every[(groups + s) * rows : (groups + s + 1) * rows, :] = other[s, 0:rows, :]
    slot = lax.broadcasted_iota(jnp.int32, (1, slots), 1)
    peer = slot // cap
    base = (((peer // 2) ^ z) + groups * ((peer & 1) ^ c)) * rows
    place = lax.broadcasted_iota(jnp.int32, (2 * groups * rows, slots), 0)
    entry = lax.broadcasted_iota(jnp.int32, (table.shape[0], rows), 0)
    for s in range(groups):
        wanted = mine[s, info + 6 : info + 7, 0:slots].astype(F32).astype(jnp.int32) + base
        pick = jnp.where(place == wanted, 1.0, 0.0).astype(BF16)
        halo = lax.dot_general(pick, every[...], ROWS_CONTRACT, preferred_element_type=F32)
        table[0:rows, :] = mine[s, 0:rows, :]
        table[rows : rows + slots, :] = halo.astype(BF16)
        table[rows + slots :, :] = jnp.zeros((table.shape[0] - rows - slots, table.shape[1]), BF16)
        out[0, s * rows : (s + 1) * rows, :] = mine[s, 0:rows, :]
        for k in range(6):
            pair = mine[s, info + k : info + k + 1, :].astype(F32).astype(jnp.int32)
            index = pair[:, 0:rows] * 32 + pair[:, rows : 2 * rows]
            pick = jnp.where(entry == index, 1.0, 0.0).astype(BF16)
            row = lax.dot_general(pick, table[...], ROWS_CONTRACT, preferred_element_type=F32)
            out[k + 1, s * rows : (s + 1) * rows, :] = row.astype(BF16)


def conv_kernel(groups, parts, rows, counts, taps, gain, *refs):
    z, c, d = spot()
    live = [counts[0, 2 * (z ^ s) + c] for s in range(groups)]
    own, beside, near, far, own_other, beside_other, near_other, far_other = refs[0:8]
    hidden_out, projected_out, summary_out, weight, proj, hidden, normed = refs[8:]
    count_taps, _, out_width = weight.shape
    depth = weight.shape[1] // (2 * groups)
    pdepth = proj.shape[0] // (2 * groups)
    cut = near.shape[2]
    strip = pdepth * cut // out_width
    width = projected_out.shape[1] // 3
    middle = count_taps * depth

    def at(row, size):
        return pl.ds(pl.multiple_of(row, size), size)

    def whole(piece, shard):
        for k in range(count_taps):
            weight[k, at(shard * depth, depth), :] = piece[k * depth : (k + 1) * depth, :]
        proj[at(shard * pdepth, pdepth), 0:out_width] = piece[middle : middle + pdepth, :]
        for i in range(parts):
            proj[at(shard * pdepth + i * strip, strip), out_width : out_width + cut] = piece[
                middle + pdepth :, i * cut : (i + 1) * cut
            ]

    def quarter(piece, shard, i):
        lanes = at(i * cut, cut)
        for k in range(count_taps):
            weight[k, at(shard * depth, depth), lanes] = piece[k * depth : (k + 1) * depth, :]
        proj[at(shard * pdepth, pdepth), lanes] = piece[middle : middle + pdepth, :]
        proj[at(shard * pdepth + i * strip, strip), out_width : out_width + cut] = piece[middle + pdepth :, :]

    for core, mine in ((c, (own, beside, near, far)), (1 - c, (own_other, beside_other, near_other, far_other))):
        whole(mine[0], 2 * z + core)
        whole(mine[1], 2 * (z ^ 1) + core)
        for k in range(2, groups):
            shard = 2 * (z ^ k) + core
            quarter(mine[2].at[k - 2], shard, d)
            for m in range(1, parts):
                quarter(mine[3].at[m - 1, k - 2], shard, d ^ m)
    total = jnp.dot(taps[0], weight[0], preferred_element_type=F32)
    for k in range(1, count_taps):
        total = total + jnp.dot(taps[k], weight[k], preferred_element_type=F32)
    hidden[...] = total
    place = lax.broadcasted_iota(jnp.int32, (rows, 1), 0)
    for s in range(groups):
        band = slice(s * rows, (s + 1) * rows)
        h = jnp.where(place < live[s], hidden[band, :], 0.0)
        if s == 0:
            hidden_out[...] = h
        power = jnp.mean(h * h, axis=-1, keepdims=True)
        normed[band, :] = (h * lax.rsqrt(power + 1e-06) * gain[...]).astype(BF16)
    projected_out[...] = jnp.dot(
        normed[...], proj[:, 0 : 3 * width], preferred_element_type=F32
    ).astype(BF16)
    blocks = groups * rows // BLK
    block = lax.broadcasted_iota(jnp.int32, (blocks, groups * rows), 0)
    token = lax.broadcasted_iota(jnp.int32, (blocks, groups * rows), 1)
    shard = lax.broadcasted_iota(jnp.int32, (blocks, 1), 0) // (rows // BLK)
    count = jnp.zeros((blocks, 1), jnp.int32)
    for s in range(groups):
        count = jnp.where(shard == s, live[s], count)
    member = (token // BLK == block) & (token - shard * rows < count)
    member = jnp.where(member, 1.0, 0.0)
    divisor = jnp.maximum(jnp.sum(member, axis=1, keepdims=True), 1.0)
    sums = jnp.dot(
        member.astype(BF16), projected_out[:, width : 3 * width], preferred_element_type=F32
    )
    summary_out[...] = (sums / divisor).astype(BF16)


def attend_kernel(groups, heads, rows, shards, info, counts, projected, mine, other, packed, attended,
                  keep, near_s, far_s, value_s, far_value_s):
    z, c, _ = spot()
    width = heads * HEAD_DIM
    short = jnp.concatenate([mine[...].astype(F32), other[...].astype(F32)], axis=0)
    slots = short.shape[0]
    keep[...] = jnp.zeros_like(keep)
    keep[0:slots, :] = short.astype(BF16)
    scale = HEAD_DIM ** (-0.5)
    across = lax.broadcasted_iota(jnp.int32, (rows, rows), 1)
    down = lax.broadcasted_iota(jnp.int32, (rows, rows), 0)
    same = across // BLK == down // BLK
    place = lax.broadcasted_iota(jnp.int32, (rows, 1), 0)
    local_blocks = rows // BLK
    picks = (local_blocks * SEL, 128)
    diagonal = lax.broadcasted_iota(jnp.int32, picks, 0) == lax.broadcasted_iota(jnp.int32, picks, 1)
    slot = lax.broadcasted_iota(jnp.int32, (1, keep.shape[0]), 1)
    shard = slot // local_blocks
    core = jnp.where(shard < groups, c, 1 - c)
    named = (2 * ((shard % groups) ^ z) + core) * local_blocks + slot % local_blocks
    named = jnp.where(slot < slots, named, -1)
    for n, s in enumerate(shards):
        band = slice(s * rows, (s + 1) * rows)
        open_keys = same & (across < counts[0, 2 * (z ^ s) + c])
        entries = packed[s, info : info + 1, 0:128].astype(F32)
        entries = jnp.sum(jnp.where(diagonal, entries, 0.0), axis=1, keepdims=True)
        hits = jnp.where(entries.astype(jnp.int32) == named, 0.0, NEG)
        far_bias = jnp.concatenate(
            [
                jnp.broadcast_to(
                    jnp.max(hits[b * SEL : (b + 1) * SEL, :], axis=0, keepdims=True), (BLK, named.shape[1])
                )
                for b in range(local_blocks)
            ],
            axis=0,
        )
        for h in range(heads):
            lane = slice(h * HEAD_DIM, (h + 1) * HEAD_DIM)
            query = projected[band, lane]
            key = projected[band, width + h * HEAD_DIM : width + (h + 1) * HEAD_DIM]
            near = lax.dot_general(query, key, LANES_CONTRACT, preferred_element_type=F32) * scale
            near_s[n * heads + h] = jnp.where(open_keys, near, NEG)
            far = lax.dot_general(query, keep[:, lane], LANES_CONTRACT, preferred_element_type=F32)
            far_s[n * heads + h] = far * scale + far_bias
    near = near_s[...]
    far = far_s[...]
    highest = jnp.max(jnp.maximum(near, far), axis=-1, keepdims=True)
    near = jnp.exp(near - highest)
    far = jnp.exp(far - highest)
    share = 1.0 / jnp.sum(near + far, axis=-1, keepdims=True)
    value_s[...] = (near * share).astype(BF16)
    far_value_s[...] = (far * share).astype(BF16)
    for n, s in enumerate(shards):
        band = slice(s * rows, (s + 1) * rows)
        live = place < counts[0, 2 * (z ^ s) + c]
        for h in range(heads):
            value = projected[band, 2 * width + h * HEAD_DIM : 2 * width + (h + 1) * HEAD_DIM]
            far_value = keep[:, width + h * HEAD_DIM : width + (h + 1) * HEAD_DIM]
            mixed = jnp.dot(value_s[n * heads + h], value, preferred_element_type=F32) + jnp.dot(
                far_value_s[n * heads + h], far_value, preferred_element_type=F32
            )
            attended[n * rows : (n + 1) * rows, h * HEAD_DIM : (h + 1) * HEAD_DIM] = jnp.where(
                live, mixed, 0.0
            ).astype(BF16)


def outer_weights(c, own, own_other, outw):
    half = own.shape[0]
    outw[pl.ds(pl.multiple_of(c * half, half), half), :] = own[...]
    outw[pl.ds(pl.multiple_of((1 - c) * half, half), half), :] = own_other[...]


def first_kernel(groups, heads, rows, info, counts, projected, mine, other, packed, own, own_other, *refs):
    shards = range(groups // 2, groups)
    shares, attended = refs[: len(shards)], refs[len(shards)]
    outw, scratch = refs[len(shards) + 1], refs[len(shards) + 2 :]
    outer_weights(spot()[1], own, own_other, outw)
    attend_kernel(groups, heads, rows, shards, info, counts, projected, mine, other, packed, attended,
                  *scratch)
    for n in range(len(shards)):
        share = jnp.dot(attended[n * rows : (n + 1) * rows, :], outw[...], preferred_element_type=F32)
        shares[n][...] = share.astype(BF16)


def second_kernel(groups, heads, rows, info, counts, projected, mine, other, packed, own, own_other,
                  early, hidden, *refs):
    shards = range(groups // 2)
    cotangent, refs = refs[:groups], refs[groups:]
    base_out, grad_out, send_out = refs[0:3]
    shares = refs[3 : 2 + len(shards)]
    outw, attended, grad = refs[2 + len(shards) : 5 + len(shards)]
    c = spot()[1]
    half = own.shape[0]
    outer_weights(c, own, own_other, outw)
    attend_kernel(groups, heads, rows, shards, info, counts, projected, mine, other, packed, attended,
                  *refs[5 + len(shards) :])
    for n in range(len(shards)):
        share = jnp.dot(attended[n * rows : (n + 1) * rows, :], outw[...], preferred_element_type=F32)
        if n == 0:
            base_out[...] = hidden[...] + share
        else:
            shares[n - 1][...] = share.astype(BF16)
    total = None
    for s in range(groups):
        source, n = (attended, s) if s < groups // 2 else (early, s - groups // 2)
        term = lax.dot_general(
            source[n * rows : (n + 1) * rows, :], cotangent[s][...], ROWS_CONTRACT, preferred_element_type=F32
        )
        total = term if total is None else total + term
    grad[...] = total
    grad_out[...] = grad[pl.ds(pl.multiple_of(c * half, half), half), :]
    send_out[...] = grad[pl.ds(pl.multiple_of((1 - c) * half, half), half), :].astype(BF16)


def finish_kernel(count, factor, base, grad, *refs):
    shares, terms = refs[:count], refs[count:-2]
    layer_out, grad_out = refs[-2:]
    layer = base[...]
    for share in shares:
        layer = layer + share[...].astype(F32)
    layer_out[...] = layer.astype(BF16)
    sums = [grad[...].astype(F32)] + [term[...].astype(F32) for term in terms]
    while len(sums) > 1:
        sums = [sums[i] + sums[i + 1] for i in range(0, len(sums), 2)]
    grad_out[...] = sums[0] * factor


def paired_shards(
    voxel_feats,
    neighbours,
    wanted_rows,
    live_counts,
    block_choice,
    conv_weight,
    norm_gain,
    input_weight,
    output_weight,
    cotangent,
):
    space = lax.axis_size("space")
    parts = lax.axis_size("dp")
    groups = space // 2
    rows, cin = voxel_feats.shape[1:]
    taps = neighbours.shape[2]
    cap = wanted_rows.shape[3]
    depth, out_width = conv_weight.shape[1:]
    pdepth = input_weight.shape[0]
    att = input_weight.shape[1] // 3
    width = att // groups
    heads = width // HEAD_DIM
    local_blocks = rows // BLK
    half = output_weight.shape[0]
    cut = out_width // parts

    def over_z(x, k):
        return lax.ppermute(x, "space", [(i, ((i // 2) ^ k) * 2 + i % 2) for i in range(space)])

    def over_core(x):
        return lax.ppermute(x, "space", [(i, i ^ 1) for i in range(space)])

    def over_dp(x, m):
        return lax.ppermute(x, "dp", [(i, i ^ m) for i in range(parts)])

    slots = space * cap
    info_rows = -(-(taps + 2) // 8) * 8
    strip = pdepth // parts
    depth_all = (taps + 1) * depth + pdepth + strip
    voxels, own, beside, *quarters = call(
        functools.partial(pack_kernel, groups, width, rows),
        [],
        [
            voxel_feats[0],
            neighbours.transpose(2, 0, 1),
            wanted_rows[0, 0],
            block_choice[0],
            input_weight,
            conv_weight,
        ],
        [jax.ShapeDtypeStruct((rows + info_rows, cin), BF16)]
        + [jax.ShapeDtypeStruct((depth_all, out_width), BF16)] * 2
        + [jax.ShapeDtypeStruct((depth_all, cut), BF16)] * (groups - 2),
        [
            pltpu.VMEM((taps, 1, rows), jnp.int32),
            pltpu.VMEM(wanted_rows.shape[2:], jnp.int32),
            pltpu.VMEM(block_choice.shape[1:], jnp.int32),
            pltpu.VMEM(input_weight.shape, BF16),
            pltpu.VMEM(conv_weight.shape, BF16),
            pltpu.VMEM((groups, pdepth + strip, out_width), BF16),
            pltpu.VMEM((info_rows, cin), F32),
            pltpu.SemaphoreType.DMA((6,)),
        ],
        1000,
        pltpu.HBM,
        PACK_LIMIT,
    )
    beside = over_z(beside, 1)
    near = jnp.stack([over_z(quarters[k - 2], k) for k in range(2, groups)])
    mine = jnp.stack([voxels] + [over_z(voxels, k) for k in range(1, groups)])
    far = jnp.stack([over_dp(near, m) for m in range(1, parts)])
    own_other = over_core(own)
    out_other = over_core(output_weight)
    beside_other = over_core(beside)
    near_other = over_core(near)
    other = over_core(mine)
    far_other = over_core(far)
    cots = [cotangent[0]] + [over_z(cotangent[0], k) for k in range(1, groups)]

    tokens = groups * rows
    table_rows = -(-(rows + slots + 1) // 128) * 128
    (gathered,) = call(
        functools.partial(taps_kernel, groups, rows, cap, rows),
        [],
        [mine, other],
        [jax.ShapeDtypeStruct((taps + 1, tokens, cin), BF16)],
        [pltpu.VMEM((2 * tokens, cin), BF16), pltpu.VMEM((table_rows, cin), BF16)],
        2 * taps * tokens * table_rows * cin,
    )
    hidden, projected, summary = call(
        functools.partial(conv_kernel, groups, parts, rows),
        [live_counts],
        [
            gathered,
            norm_gain[None, :],
            own,
            beside,
            near,
            far,
            own_other,
            beside_other,
            near_other,
            far_other,
        ],
        [
            jax.ShapeDtypeStruct((rows, out_width), F32),
            jax.ShapeDtypeStruct((tokens, 3 * width), BF16),
            jax.ShapeDtypeStruct((groups * local_blocks, 2 * width), BF16),
        ],
        [
            pltpu.VMEM((taps + 1, cin, out_width), BF16),
            pltpu.VMEM((space * pdepth, -(-3 * width // 128) * 128), BF16),
            pltpu.VMEM((tokens, out_width), F32),
            pltpu.VMEM((tokens, out_width), BF16),
        ],
        2 * tokens * out_width * ((taps + 1) * cin + 3 * width),
    )
    summary_other = over_core(summary)

    near_shards = groups // 2
    far_shards = groups - near_shards
    share = jax.ShapeDtypeStruct((rows, out_width), BF16)
    padded = -(-space * local_blocks // 128) * 128
    outer = pltpu.VMEM((2 * half, out_width), BF16)

    def softmax_space(shards):
        return [
            pltpu.VMEM((padded, 2 * width), BF16),
            pltpu.VMEM((shards * heads, rows, rows), F32),
            pltpu.VMEM((shards * heads, rows, padded), F32),
            pltpu.VMEM((shards * heads, rows, rows), BF16),
            pltpu.VMEM((shards * heads, rows, padded), BF16),
        ]

    common = [projected, summary, summary_other, mine, output_weight, out_other]
    *shares, early = call(
        functools.partial(first_kernel, groups, heads, rows, rows + taps + 1),
        [live_counts],
        common,
        [share] * far_shards + [jax.ShapeDtypeStruct((far_shards * rows, width), BF16)],
        [outer] + softmax_space(far_shards),
        4 * tokens * width * (rows + out_width),
    )
    received = [over_z(shares[k - near_shards], k) for k in range(near_shards, groups)]
    base, grad, send, *shares = call(
        functools.partial(second_kernel, groups, heads, rows, rows + taps + 1),
        [live_counts],
        common + [early, hidden, *cots],
        [
            jax.ShapeDtypeStruct((rows, out_width), F32),
            jax.ShapeDtypeStruct((half, out_width), F32),
            jax.ShapeDtypeStruct((half, out_width), BF16),
        ]
        + [share] * (near_shards - 1),
        [
            outer,
            pltpu.VMEM((near_shards * rows, width), BF16),
            pltpu.VMEM((2 * half, out_width), F32),
        ]
        + softmax_space(near_shards),
        6 * tokens * width * (rows + out_width),
    )
    received += [over_z(shares[k - 1], k) for k in range(1, near_shards)]
    grad = (grad + over_core(send).astype(F32)).astype(BF16)
    terms = [over_dp(grad, m) for m in range(1, parts)]
    factor = (parts * space * rows) ** (-0.5)
    layer, total = call(
        functools.partial(finish_kernel, len(received), factor),
        [],
        [base, grad, *received, *terms],
        [share, jax.ShapeDtypeStruct((half, out_width), F32)],
        [],
        1000,
    )
    return (layer[None], total)


def section(mesh, *args):
    space, parts = mesh.shape["space"], mesh.shape["dp"]
    groups = space // 2
    powers = space % 2 == 0 and groups & (groups - 1) == 0 and parts & (parts - 1) == 0
    rows, cin = args[0].shape[1:]
    depth, out_width = args[5].shape[1:]
    pdepth = args[7].shape[0]
    width = args[7].shape[1] // 3 // groups if groups else 0
    cut = out_width // parts
    fits = (
        powers
        and groups >= 4
        and HEADS % groups == 0
        and out_width % (128 * parts) == 0
        and 0 < 3 * width - out_width <= cut
        and pdepth % (16 * parts) == 0
        and depth % 32 == 0
        and rows * 2 == cin
        and space * args[2].shape[3] <= rows
    )
    if not fits:
        return general_shards(*args)
    return paired_shards(*args)


def solution(mesh):
    placed = (
        P("dp", "space", None),
        P("dp", "space", None),
        P("dp", "space", None, None),
        P("dp", None),
        P("dp", "space", None),
        P(None, "space", None),
        P(),
        P("space", None),
        P("space", None),
        P("dp", "space", None),
    )
    return jax.shard_map(
        functools.partial(section, mesh),
        mesh=mesh,
        in_specs=placed,
        out_specs=(P("dp", "space", None), P("space", None)),
        check_vma=False,
    )
```

```python
import functools

import jax
import jax.numpy as jnp
from jax import lax
from jax.experimental import pallas as pl
from jax.experimental.pallas import tpu as pltpu
from jax.sharding import PartitionSpec as P


HEADS = 12
HEAD_DIM = 64
BLK = 64
SEL = 4


def attend(query, keys, values, key_live, short_keys, short_values):
    scale = HEAD_DIM ** (-0.5)
    near = jnp.einsum("bqhd,bkhd->bhqk", query, keys, preferred_element_type=jnp.float32) * scale
    near = jnp.where(key_live[:, None, None, :], near, -1e30)
    far = (
        jnp.einsum("bqhd,bshd->bhqs", query, short_keys, preferred_element_type=jnp.float32) * scale
    )
    scores = jnp.concatenate([near, far], axis=-1)
    highest = jnp.max(scores, axis=-1, keepdims=True)
    weights = jnp.exp(scores - highest)
    weights = (weights / jnp.sum(weights, axis=-1, keepdims=True)).astype(jnp.bfloat16)
    mixed = jnp.einsum(
        "bhqk,bkhd->bqhd", weights[..., :BLK], values, preferred_element_type=jnp.float32
    )
    return mixed + jnp.einsum(
        "bhqs,bshd->bqhd", weights[..., BLK:], short_values, preferred_element_type=jnp.float32
    )


def general_shards(
    voxel_feats,
    neighbours,
    wanted_rows,
    live_counts,
    block_choice,
    conv_weight,
    norm_gain,
    input_weight,
    output_weight,
    cotangent,
):
    space_count = lax.axis_size("space")
    position = lax.axis_index("space")
    own_rows = voxel_feats[0]
    shard_rows = own_rows.shape[0]
    index_map = neighbours[0]
    zero_row = jnp.zeros((1, own_rows.shape[1]), jnp.bfloat16)
    requested = lax.all_to_all(wanted_rows[0, 0], "space", split_axis=0, concat_axis=0, tiled=True)
    answers = own_rows[requested]
    arrived = lax.all_to_all(answers, "space", split_axis=0, concat_axis=0, tiled=True)
    padded = jnp.concatenate([own_rows, arrived.reshape(-1, own_rows.shape[1]), zero_row], axis=0)
    gathered_taps = padded[index_map]
    table = jnp.concatenate([own_rows[:, None, :], gathered_taps], axis=1)
    columns = table
    hidden = jnp.einsum(
        "tkr,kro->to",
        columns,
        lax.all_gather(conv_weight, "space", axis=1, tiled=True),
        preferred_element_type=jnp.float32,
    )
    live_count = lax.dynamic_index_in_dim(live_counts[0], position, keepdims=False)
    live = jnp.arange(shard_rows, dtype=jnp.int32) < live_count
    live_f = live.astype(jnp.float32)
    hidden = hidden * live_f[:, None]
    power = jnp.mean(hidden * hidden, axis=-1, keepdims=True)
    normed = (hidden * lax.rsqrt(power + 1e-06) * norm_gain).astype(jnp.bfloat16)
    columns = normed
    projected = jnp.dot(
        columns,
        lax.all_gather(input_weight, "space", axis=0, tiled=True),
        preferred_element_type=jnp.float32,
    ).astype(jnp.bfloat16)
    att_width = input_weight.shape[1] // 3
    local_blocks = shard_rows // BLK
    query = projected[:, :att_width].reshape(local_blocks, BLK, HEADS, HEAD_DIM)
    keys = projected[:, att_width : 2 * att_width]
    values = projected[:, 2 * att_width :]
    block_live = live_f.reshape(local_blocks, BLK)
    divisor = jnp.maximum(jnp.sum(block_live, axis=1), 1.0)[:, None]
    short_keys = (
        jnp.sum(
            keys.astype(jnp.float32).reshape(local_blocks, BLK, att_width) * block_live[:, :, None],
            axis=1,
        )
        / divisor
    ).astype(jnp.bfloat16)
    short_values = (
        jnp.sum(
            values.astype(jnp.float32).reshape(local_blocks, BLK, att_width)
            * block_live[:, :, None],
            axis=1,
        )
        / divisor
    ).astype(jnp.bfloat16)
    every_keys, every_values = (
        lax.all_gather(short_keys, "space", axis=0, tiled=True),
        lax.all_gather(short_values, "space", axis=0, tiled=True),
    )
    chosen = block_choice[0]
    picked_keys = every_keys[chosen].reshape(local_blocks, SEL, HEADS, HEAD_DIM)
    picked_values = every_values[chosen].reshape(local_blocks, SEL, HEADS, HEAD_DIM)
    mixed = attend(
        query,
        keys.reshape(local_blocks, BLK, HEADS, HEAD_DIM),
        values.reshape(local_blocks, BLK, HEADS, HEAD_DIM),
        live.reshape(local_blocks, BLK),
        picked_keys,
        picked_values,
    )
    attended = (mixed.reshape(shard_rows, att_width) * live_f[:, None]).astype(jnp.bfloat16)
    columns = attended
    projected_out = jnp.dot(
        columns,
        lax.all_gather(output_weight, "space", axis=0, tiled=True),
        preferred_element_type=jnp.float32,
    )
    layer = (hidden + projected_out).astype(jnp.bfloat16)[None]
    upstream = cotangent[0]
    factor = (lax.axis_size("dp") * space_count * shard_rows) ** (-0.5)
    shard_sum = lax.psum_scatter(
        jnp.dot(attended.T, upstream, preferred_element_type=jnp.float32).astype(jnp.bfloat16),
        "space",
        scatter_dimension=0,
        tiled=True,
    )
    gradient = lax.psum(shard_sum, "dp").astype(jnp.float32)
    return (layer, gradient * factor)


NEG = -1e30
F32 = jnp.float32
PACK_LIMIT = 24000000
BF16 = jnp.bfloat16
ROWS_CONTRACT = (((0,), (0,)), ((), ()))
LANES_CONTRACT = (((1,), (1,)), ((), ()))


def spot():
    position = lax.axis_index("space")
    return position // 2, position % 2, lax.axis_index("dp")


def vmem():
    return pl.BlockSpec(memory_space=pltpu.VMEM)


def smem():
    return pl.BlockSpec(memory_space=pltpu.SMEM)


def call(kernel, scalars, arrays, outs, scratch, flops, space=pltpu.VMEM, limit=24 * 2**20):
    size = sum(a.size * a.dtype.itemsize for a in list(arrays) + list(outs))
    return pl.pallas_call(
        kernel,
        out_shape=tuple(outs),
        in_specs=[smem()] * len(scalars) + [pl.BlockSpec(memory_space=space)] * len(arrays),
        out_specs=tuple(vmem() for _ in outs),
        scratch_shapes=scratch,
        compiler_params=pltpu.CompilerParams(vmem_limit_bytes=limit),
        cost_estimate=pl.CostEstimate(flops=flops, bytes_accessed=size, transcendentals=0),
    )(*scalars, *([pltpu.with_memory_space_constraint(x, space) for x in arrays] if space == pltpu.HBM else arrays))


def pack_kernel(groups, width, rows, feats_in, near_in, wanted_in, chosen_in, weight_in, conv_in, cot_in,
                *refs):
    voxels, own, beside = refs[0:3]
    quarters = refs[3 : groups + 1]
    cot, near, wanted, chosen, weight, conv, pieces, info, sems = refs[groups + 1 :]
    z, _, d = spot()
    copies = [
        pltpu.make_async_copy(source, target, sems.at[i])
        for i, (source, target) in enumerate(
            (
                (weight_in, weight),
                (conv_in, conv),
                (feats_in, voxels.at[pl.ds(0, rows)]),
                (near_in, near),
                (wanted_in, wanted),
                (chosen_in, chosen),
                (cot_in, cot),
            )
        )
    ]
    for copy in copies:
        copy.start()
    info[...] = jnp.zeros_like(info)
    copies[0].wait()
    depth = weight.shape[0]
    att = weight.shape[1] // 3
    taps, cdepth, out_width = conv.shape
    cut = quarters[0].shape[1]
    strip = depth * cut // out_width
    tail = 3 * width - out_width
    blank = jnp.zeros((depth, cut - tail), BF16)
    for group in range(groups):
        parts = [weight[:, p * att + group * width : p * att + (group + 1) * width] for p in range(3)]
        piece = jnp.concatenate(parts + [blank], axis=1)
        pieces[z ^ group, 0:depth, :] = piece[:, 0:out_width]
        for i in range(depth // strip):
            pieces[z ^ group, depth : depth + strip, i * cut : (i + 1) * cut] = piece[
                i * strip : (i + 1) * strip, out_width:
            ]
    lanes = pl.ds(pl.multiple_of(d * cut, cut), cut)
    copies[1].wait()
    for k in range(taps):
        band = slice(k * cdepth, (k + 1) * cdepth)
        own[band, :] = conv[k]
        beside[band, :] = conv[k]
        mine = conv[k, :, lanes]
        for quarter in quarters:
            quarter[band, :] = mine
    own[taps * cdepth :, :] = pieces[0]
    beside[taps * cdepth :, :] = pieces[1]
    for i, quarter in enumerate(quarters):
        quarter[taps * cdepth :, :] = pieces[2 + i, :, lanes]
    for copy in copies[2:]:
        copy.wait()
    for k in range(near.shape[0]):
        high = near[k] // 32
        info[k : k + 1, 0:rows] = high.astype(F32)
        info[k : k + 1, rows : 2 * rows] = (near[k] - high * 32).astype(F32)
    count = near.shape[0]
    cap = wanted.shape[1]
    for p in range(wanted.shape[0]):
        info[count : count + 1, p * cap : (p + 1) * cap] = wanted[p : p + 1, :].astype(F32)
    for b in range(chosen.shape[0]):
        info[count + 1 : count + 2, b * SEL : (b + 1) * SEL] = chosen[b : b + 1, :].astype(F32)
    voxels[rows:, :] = info[...].astype(BF16)


def taps_kernel(groups, rows, cap, info, mine, other, out, every, table):
    z, c, _ = spot()
    slots = 2 * groups * cap
    for s in range(groups):
        every[s * rows : (s + 1) * rows, :] = mine[s, 0:rows, :]
        every[(groups + s) * rows : (groups + s + 1) * rows, :] = other[s, 0:rows, :]
    slot = lax.broadcasted_iota(jnp.int32, (1, slots), 1)
    peer = slot // cap
    base = (((peer // 2) ^ z) + groups * ((peer & 1) ^ c)) * rows
    place = lax.broadcasted_iota(jnp.int32, (2 * groups * rows, slots), 0)
    entry = lax.broadcasted_iota(jnp.int32, (table.shape[0], rows), 0)
    for s in range(groups):
        wanted = mine[s, info + 6 : info + 7, 0:slots].astype(F32).astype(jnp.int32) + base
        pick = jnp.where(place == wanted, 1.0, 0.0).astype(BF16)
        halo = lax.dot_general(pick, every[...], ROWS_CONTRACT, preferred_element_type=F32)
        table[0:rows, :] = mine[s, 0:rows, :]
        table[rows : rows + slots, :] = halo.astype(BF16)
        table[rows + slots :, :] = jnp.zeros((table.shape[0] - rows - slots, table.shape[1]), BF16)
        out[0, s * rows : (s + 1) * rows, :] = mine[s, 0:rows, :]
        for k in range(6):
            pair = mine[s, info + k : info + k + 1, :].astype(F32).astype(jnp.int32)
            index = pair[:, 0:rows] * 32 + pair[:, rows : 2 * rows]
            pick = jnp.where(entry == index, 1.0, 0.0).astype(BF16)
            row = lax.dot_general(pick, table[...], ROWS_CONTRACT, preferred_element_type=F32)
            out[k + 1, s * rows : (s + 1) * rows, :] = row.astype(BF16)


def conv_kernel(groups, parts, rows, counts, taps, gain, *refs):
    z, c, d = spot()
    live = [counts[0, 2 * (z ^ s) + c] for s in range(groups)]
    own, beside, near, far, own_other, beside_other, near_other, far_other = refs[0:8]
    hidden_out, projected_out, summary_out, weight, proj, hidden, normed = refs[8:]
    count_taps, _, out_width = weight.shape
    depth = weight.shape[1] // (2 * groups)
    pdepth = proj.shape[0] // (2 * groups)
    cut = near.shape[2]
    strip = pdepth * cut // out_width
    width = projected_out.shape[1] // 3
    middle = count_taps * depth

    def at(row, size):
        return pl.ds(pl.multiple_of(row, size), size)

    def whole(piece, shard):
        for k in range(count_taps):
            weight[k, at(shard * depth, depth), :] = piece[k * depth : (k + 1) * depth, :]
        proj[at(shard * pdepth, pdepth), 0:out_width] = piece[middle : middle + pdepth, :]
        for i in range(parts):
            proj[at(shard * pdepth + i * strip, strip), out_width : out_width + cut] = piece[
                middle + pdepth :, i * cut : (i + 1) * cut
            ]

    def quarter(piece, shard, i):
        lanes = at(i * cut, cut)
        for k in range(count_taps):
            weight[k, at(shard * depth, depth), lanes] = piece[k * depth : (k + 1) * depth, :]
        proj[at(shard * pdepth, pdepth), lanes] = piece[middle : middle + pdepth, :]
        proj[at(shard * pdepth + i * strip, strip), out_width : out_width + cut] = piece[middle + pdepth :, :]

    for core, mine in ((c, (own, beside, near, far)), (1 - c, (own_other, beside_other, near_other, far_other))):
        whole(mine[0], 2 * z + core)
        whole(mine[1], 2 * (z ^ 1) + core)
        for k in range(2, groups):
            shard = 2 * (z ^ k) + core
            quarter(mine[2].at[k - 2], shard, d)
            for m in range(1, parts):
                quarter(mine[3].at[m - 1, k - 2], shard, d ^ m)
    total = jnp.dot(taps[0], weight[0], preferred_element_type=F32)
    for k in range(1, count_taps):
        total = total + jnp.dot(taps[k], weight[k], preferred_element_type=F32)
    hidden[...] = total
    place = lax.broadcasted_iota(jnp.int32, (rows, 1), 0)
    for s in range(groups):
        band = slice(s * rows, (s + 1) * rows)
        h = jnp.where(place < live[s], hidden[band, :], 0.0)
        if s == 0:
            hidden_out[...] = h
        power = jnp.mean(h * h, axis=-1, keepdims=True)
        normed[band, :] = (h * lax.rsqrt(power + 1e-06) * gain[...]).astype(BF16)
    projected_out[...] = jnp.dot(
        normed[...], proj[:, 0 : 3 * width], preferred_element_type=F32
    ).astype(BF16)
    blocks = groups * rows // BLK
    block = lax.broadcasted_iota(jnp.int32, (blocks, groups * rows), 0)
    token = lax.broadcasted_iota(jnp.int32, (blocks, groups * rows), 1)
    shard = lax.broadcasted_iota(jnp.int32, (blocks, 1), 0) // (rows // BLK)
    count = jnp.zeros((blocks, 1), jnp.int32)
    for s in range(groups):
        count = jnp.where(shard == s, live[s], count)
    member = (token // BLK == block) & (token - shard * rows < count)
    member = jnp.where(member, 1.0, 0.0)
    divisor = jnp.maximum(jnp.sum(member, axis=1, keepdims=True), 1.0)
    sums = jnp.dot(
        member.astype(BF16), projected_out[:, width : 3 * width], preferred_element_type=F32
    )
    summary_out[...] = (sums / divisor).astype(BF16)


def attend_kernel(groups, heads, rows, shards, info, counts, projected, mine, other, packed, attended,
                  keep, near_s, far_s, value_s, far_value_s):
    z, c, _ = spot()
    width = heads * HEAD_DIM
    short = jnp.concatenate([mine[...].astype(F32), other[...].astype(F32)], axis=0)
    slots = short.shape[0]
    keep[...] = jnp.zeros_like(keep)
    keep[0:slots, :] = short.astype(BF16)
    scale = HEAD_DIM ** (-0.5)
    across = lax.broadcasted_iota(jnp.int32, (rows, rows), 1)
    down = lax.broadcasted_iota(jnp.int32, (rows, rows), 0)
    same = across // BLK == down // BLK
    place = lax.broadcasted_iota(jnp.int32, (rows, 1), 0)
    local_blocks = rows // BLK
    picks = (local_blocks * SEL, 128)
    diagonal = lax.broadcasted_iota(jnp.int32, picks, 0) == lax.broadcasted_iota(jnp.int32, picks, 1)
    slot = lax.broadcasted_iota(jnp.int32, (1, keep.shape[0]), 1)
    shard = slot // local_blocks
    core = jnp.where(shard < groups, c, 1 - c)
    named = (2 * ((shard % groups) ^ z) + core) * local_blocks + slot % local_blocks
    named = jnp.where(slot < slots, named, -1)
    for n, s in enumerate(shards):
        band = slice(s * rows, (s + 1) * rows)
        open_keys = same & (across < counts[0, 2 * (z ^ s) + c])
        entries = packed[s, info : info + 1, 0:128].astype(F32)
        entries = jnp.sum(jnp.where(diagonal, entries, 0.0), axis=1, keepdims=True)
        hits = jnp.where(entries.astype(jnp.int32) == named, 0.0, NEG)
        far_bias = jnp.concatenate(
            [
                jnp.broadcast_to(
                    jnp.max(hits[b * SEL : (b + 1) * SEL, :], axis=0, keepdims=True), (BLK, named.shape[1])
                )
                for b in range(local_blocks)
            ],
            axis=0,
        )
        for h in range(heads):
            lane = slice(h * HEAD_DIM, (h + 1) * HEAD_DIM)
            query = projected[band, lane]
            key = projected[band, width + h * HEAD_DIM : width + (h + 1) * HEAD_DIM]
            near = lax.dot_general(query, key, LANES_CONTRACT, preferred_element_type=F32) * scale
            near_s[n * heads + h] = jnp.where(open_keys, near, NEG)
            far = lax.dot_general(query, keep[:, lane], LANES_CONTRACT, preferred_element_type=F32)
            far_s[n * heads + h] = far * scale + far_bias
    near = near_s[...]
    far = far_s[...]
    highest = jnp.max(jnp.maximum(near, far), axis=-1, keepdims=True)
    near = jnp.exp(near - highest)
    far = jnp.exp(far - highest)
    share = 1.0 / jnp.sum(near + far, axis=-1, keepdims=True)
    value_s[...] = (near * share).astype(BF16)
    far_value_s[...] = (far * share).astype(BF16)
    for n, s in enumerate(shards):
        band = slice(s * rows, (s + 1) * rows)
        live = place < counts[0, 2 * (z ^ s) + c]
        for h in range(heads):
            value = projected[band, 2 * width + h * HEAD_DIM : 2 * width + (h + 1) * HEAD_DIM]
            far_value = keep[:, width + h * HEAD_DIM : width + (h + 1) * HEAD_DIM]
            mixed = jnp.dot(value_s[n * heads + h], value, preferred_element_type=F32) + jnp.dot(
                far_value_s[n * heads + h], far_value, preferred_element_type=F32
            )
            attended[n * rows : (n + 1) * rows, h * HEAD_DIM : (h + 1) * HEAD_DIM] = jnp.where(
                live, mixed, 0.0
            ).astype(BF16)


def outer_weights(c, own, own_other, outw):
    half = own.shape[0]
    outw[pl.ds(pl.multiple_of(c * half, half), half), :] = own[...]
    outw[pl.ds(pl.multiple_of((1 - c) * half, half), half), :] = own_other[...]


def first_kernel(groups, heads, rows, info, counts, projected, mine, other, packed, own, own_other, *refs):
    shards = range(groups // 2, groups)
    shares, attended = refs[: len(shards)], refs[len(shards)]
    outw, scratch = refs[len(shards) + 1], refs[len(shards) + 2 :]
    outer_weights(spot()[1], own, own_other, outw)
    attend_kernel(groups, heads, rows, shards, info, counts, projected, mine, other, packed, attended,
                  *scratch)
    for n in range(len(shards)):
        share = jnp.dot(attended[n * rows : (n + 1) * rows, :], outw[...], preferred_element_type=F32)
        shares[n][...] = share.astype(BF16)


def second_kernel(groups, heads, rows, info, counts, projected, mine, other, packed, own, own_other,
                  early, hidden, *refs):
    shards = range(groups // 2)
    own_cot, beside_cot, crossed, passed = refs[0:4]
    refs = refs[4:]
    base_out, grad_out, send_out = refs[0:3]
    shares = refs[3 : 2 + len(shards)]
    outw, attended, grad = refs[2 + len(shards) : 5 + len(shards)]
    c = spot()[1]
    half = own.shape[0]
    outer_weights(c, own, own_other, outw)
    attend_kernel(groups, heads, rows, shards, info, counts, projected, mine, other, packed, attended,
                  *refs[5 + len(shards) :])
    for n in range(len(shards)):
        share = jnp.dot(attended[n * rows : (n + 1) * rows, :], outw[...], preferred_element_type=F32)
        if n == 0:
            base_out[...] = hidden[...] + share
        else:
            shares[n - 1][...] = share.astype(BF16)
    z = spot()[0]
    outside = (z == 0) | (z == groups - 1)
    place = jnp.where(outside, 0, 1)
    cots = [own_cot[...], beside_cot[...]]
    for i in (place, 1 - place):
        cots.append(jnp.where(outside, passed[i], crossed[i]))
    total = None
    for s in range(groups):
        source, n = (attended, s) if s < groups // 2 else (early, s - groups // 2)
        term = lax.dot_general(
            source[n * rows : (n + 1) * rows, :], cots[s], ROWS_CONTRACT, preferred_element_type=F32
        )
        total = term if total is None else total + term
    grad[...] = total
    grad_out[...] = grad[pl.ds(pl.multiple_of(c * half, half), half), :]
    send_out[...] = grad[pl.ds(pl.multiple_of((1 - c) * half, half), half), :].astype(BF16)


def finish_kernel(count, factor, base, grad, *refs):
    shares, terms = refs[:count], refs[count:-2]
    layer_out, grad_out = refs[-2:]
    layer = base[...]
    for share in shares:
        layer = layer + share[...].astype(F32)
    layer_out[...] = layer.astype(BF16)
    sums = [grad[...].astype(F32)] + [term[...].astype(F32) for term in terms]
    while len(sums) > 1:
        sums = [sums[i] + sums[i + 1] for i in range(0, len(sums), 2)]
    grad_out[...] = sums[0] * factor


def paired_shards(
    voxel_feats,
    neighbours,
    wanted_rows,
    live_counts,
    block_choice,
    conv_weight,
    norm_gain,
    input_weight,
    output_weight,
    cotangent,
):
    space = lax.axis_size("space")
    parts = lax.axis_size("dp")
    groups = space // 2
    rows, cin = voxel_feats.shape[1:]
    taps = neighbours.shape[2]
    cap = wanted_rows.shape[3]
    depth, out_width = conv_weight.shape[1:]
    pdepth = input_weight.shape[0]
    att = input_weight.shape[1] // 3
    width = att // groups
    heads = width // HEAD_DIM
    local_blocks = rows // BLK
    half = output_weight.shape[0]
    cut = out_width // parts

    def over_z(x, k):
        return lax.ppermute(x, "space", [(i, ((i // 2) ^ k) * 2 + i % 2) for i in range(space)])

    def over_core(x):
        return lax.ppermute(x, "space", [(i, i ^ 1) for i in range(space)])

    def over_dp(x, m):
        return lax.ppermute(x, "dp", [(i, i ^ m) for i in range(parts)])

    slots = space * cap
    info_rows = -(-(taps + 2) // 8) * 8
    strip = pdepth // parts
    depth_all = (taps + 1) * depth + pdepth + strip
    voxels, own, beside, *quarters, own_cot = call(
        functools.partial(pack_kernel, groups, width, rows),
        [],
        [
            voxel_feats[0],
            neighbours.transpose(2, 0, 1),
            wanted_rows[0, 0],
            block_choice[0],
            input_weight,
            conv_weight,
            cotangent[0],
        ],
        [jax.ShapeDtypeStruct((rows + info_rows, cin), BF16)]
        + [jax.ShapeDtypeStruct((depth_all, out_width), BF16)] * 2
        + [jax.ShapeDtypeStruct((depth_all, cut), BF16)] * (groups - 2)
        + [jax.ShapeDtypeStruct((rows, out_width), BF16)],
        [
            pltpu.VMEM((taps, 1, rows), jnp.int32),
            pltpu.VMEM(wanted_rows.shape[2:], jnp.int32),
            pltpu.VMEM(block_choice.shape[1:], jnp.int32),
            pltpu.VMEM(input_weight.shape, BF16),
            pltpu.VMEM(conv_weight.shape, BF16),
            pltpu.VMEM((groups, pdepth + strip, out_width), BF16),
            pltpu.VMEM((info_rows, cin), F32),
            pltpu.SemaphoreType.DMA((7,)),
        ],
        1000,
        pltpu.HBM,
        PACK_LIMIT,
    )
    beside = over_z(beside, 1)
    near = jnp.stack([over_z(quarters[k - 2], k) for k in range(2, groups)])
    mine = jnp.stack([voxels] + [over_z(voxels, k) for k in range(1, groups)])
    far = [over_dp(near, m) for m in range(1, parts)]
    far = jnp.stack(far)
    own_other = over_core(own)
    out_other = over_core(output_weight)
    beside_other = over_core(beside)
    near_other = over_core(near)
    other = over_core(mine)
    far_other = over_core(far)
    beside_cot = over_z(own_cot, 1)
    pair = jnp.stack([own_cot, beside_cot])
    low, high = groups // 2 - 1, groups // 2
    inner = [(2 * a + i, 2 * b + i) for i in range(2) for a, b in ((low, high), (high, low))]
    outer = [(2 * a + i, 2 * b + i) for i in range(2) for a, b in ((low, low - 1), (high, high + 1))]
    crossed = lax.ppermute(pair, "space", inner)
    cots = [own_cot, beside_cot, crossed, lax.ppermute(crossed, "space", outer)]

    tokens = groups * rows
    table_rows = -(-(rows + slots + 1) // 128) * 128
    (gathered,) = call(
        functools.partial(taps_kernel, groups, rows, cap, rows),
        [],
        [mine, other],
        [jax.ShapeDtypeStruct((taps + 1, tokens, cin), BF16)],
        [pltpu.VMEM((2 * tokens, cin), BF16), pltpu.VMEM((table_rows, cin), BF16)],
        2 * taps * tokens * table_rows * cin,
    )
    hidden, projected, summary = call(
        functools.partial(conv_kernel, groups, parts, rows),
        [live_counts],
        [
            gathered,
            norm_gain[None, :],
            own,
            beside,
            near,
            far,
            own_other,
            beside_other,
            near_other,
            far_other,
        ],
        [
            jax.ShapeDtypeStruct((rows, out_width), F32),
            jax.ShapeDtypeStruct((tokens, 3 * width), BF16),
            jax.ShapeDtypeStruct((groups * local_blocks, 2 * width), BF16),
        ],
        [
            pltpu.VMEM((taps + 1, cin, out_width), BF16),
            pltpu.VMEM((space * pdepth, -(-3 * width // 128) * 128), BF16),
            pltpu.VMEM((tokens, out_width), F32),
            pltpu.VMEM((tokens, out_width), BF16),
        ],
        2 * tokens * out_width * ((taps + 1) * cin + 3 * width),
    )
    summary_other = over_core(summary)

    near_shards = groups // 2
    far_shards = groups - near_shards
    share = jax.ShapeDtypeStruct((rows, out_width), BF16)
    padded = -(-space * local_blocks // 128) * 128
    outer = pltpu.VMEM((2 * half, out_width), BF16)

    def softmax_space(shards):
        return [
            pltpu.VMEM((padded, 2 * width), BF16),
            pltpu.VMEM((shards * heads, rows, rows), F32),
            pltpu.VMEM((shards * heads, rows, padded), F32),
            pltpu.VMEM((shards * heads, rows, rows), BF16),
            pltpu.VMEM((shards * heads, rows, padded), BF16),
        ]

    common = [projected, summary, summary_other, mine, output_weight, out_other]
    *shares, early = call(
        functools.partial(first_kernel, groups, heads, rows, rows + taps + 1),
        [live_counts],
        common,
        [share] * far_shards + [jax.ShapeDtypeStruct((far_shards * rows, width), BF16)],
        [outer] + softmax_space(far_shards),
        4 * tokens * width * (rows + out_width),
    )
    received = [over_z(shares[k - near_shards], k) for k in range(near_shards, groups)]
    base, grad, send, *shares = call(
        functools.partial(second_kernel, groups, heads, rows, rows + taps + 1),
        [live_counts],
        common + [early, hidden, *cots],
        [
            jax.ShapeDtypeStruct((rows, out_width), F32),
            jax.ShapeDtypeStruct((half, out_width), F32),
            jax.ShapeDtypeStruct((half, out_width), BF16),
        ]
        + [share] * (near_shards - 1),
        [
            outer,
            pltpu.VMEM((near_shards * rows, width), BF16),
            pltpu.VMEM((2 * half, out_width), F32),
        ]
        + softmax_space(near_shards),
        6 * tokens * width * (rows + out_width),
    )
    received += [over_z(shares[k - 1], k) for k in range(1, near_shards)]
    grad = (grad + over_core(send).astype(F32)).astype(BF16)
    terms = [over_dp(grad, m) for m in range(1, parts)]
    factor = (parts * space * rows) ** (-0.5)
    layer, total = call(
        functools.partial(finish_kernel, len(received), factor),
        [],
        [base, grad, *received, *terms],
        [share, jax.ShapeDtypeStruct((half, out_width), F32)],
        [],
        1000,
    )
    return (layer[None], total)


def section(mesh, *args):
    space, parts = mesh.shape["space"], mesh.shape["dp"]
    groups = space // 2
    powers = space % 2 == 0 and groups & (groups - 1) == 0 and parts & (parts - 1) == 0
    rows, cin = args[0].shape[1:]
    depth, out_width = args[5].shape[1:]
    pdepth = args[7].shape[0]
    width = args[7].shape[1] // 3 // groups if groups else 0
    cut = out_width // parts
    fits = (
        powers
        and groups == 4
        and HEADS % groups == 0
        and out_width % (128 * parts) == 0
        and 0 < 3 * width - out_width <= cut
        and pdepth % (16 * parts) == 0
        and depth % 32 == 0
        and rows * 2 == cin
        and space * args[2].shape[3] <= rows
    )
    if not fits:
        return general_shards(*args)
    return paired_shards(*args)


def solution(mesh):
    placed = (
        P("dp", "space", None),
        P("dp", "space", None),
        P("dp", "space", None, None),
        P("dp", None),
        P("dp", "space", None),
        P(None, "space", None),
        P(),
        P("space", None),
        P("space", None),
        P("dp", "space", None),
    )
    return jax.shard_map(
        functools.partial(section, mesh),
        mesh=mesh,
        in_specs=placed,
        out_specs=(P("dp", "space", None), P("space", None)),
        check_vma=False,
    )
```
